32 devices in a mesh: section: 4 (over y, core), dom: 8 (over z, x).
Axes of the slice: x: 2, y: 2, z: 4, core: 2. Of those that a mesh axis runs over, the one named last changes fastest.
Arguments:
- initial_feat: bfloat16 [2, 2048, 1024], P(None, 'dom'), may hold values from -6 to 6
- layer_weight: bfloat16 [4, 1024, 1024], P('section'), may hold values from -1.35 to 1.35
- tile_column: int32 [8, 2, 2, 4], P('dom'), may hold values from 0 to 1, as said below
- tile_values: bfloat16 [8, 2, 2, 4, 128, 128], P('dom'), may hold values from 0 to 0.05625, as said below
- send_rows: int32 [8, 2, 8, 16], P('dom'), may hold values from 0 to 255
Outputs:
- activations: bfloat16 [4, 2, 2048, 1024], P('section', None, 'dom')
The draws below stay inside these ranges and needn't reach their ends.
Inputs may be any that keep to these rules, and one draw needn't show every extreme that they name: `tile_column`: each of the two column blocks appears in at least one of the 4 tiles of every partition, node batch and row block. `tile_values`: each row of a tile has a few nonzero weights; the weights of one row over all tiles of its row block sum to about one.
All inputs are finite; a program needn't handle non-finite values.
Results may differ from the reference program's by a relative error of at most 0.006.
Values may be sent and summed in bfloat16 or wider, within the bound.
No kernel may reach another device: no remote copies, remote signals or barrier semaphores. Data moves between devices by JAX's collectives and lax.ppermute only.
A program may use at most 64 MiB of HBM per device.

```python
import math
import jax
import jax.numpy as jnp

F = 1024
BLK = 128
ROWBLOCKS = 2
BATCHES = 2
TILES = 4
PART_ROWS = 256
PARTITIONS = 8
LAYERS = 4
SEND = 16
NODES = 2048


def draw_layer_weight(key, part):
    key_weight = jax.random.fold_in(key, 37)
    weight_shape = (LAYERS, F, F)
    layer_num = jnp.arange(1, LAYERS + 1, dtype=jnp.float32)
    beta_mix = jnp.log(0.5 / layer_num + 1.0)
    spread = (0.8 / (math.sqrt(F) * beta_mix))[:, None, None]
    random_part = jnp.clip(jax.random.normal(key_weight, weight_shape), -6.0, 6.0)
    return (random_part * spread).astype(jnp.bfloat16)


def draw_tile_column(key, part):
    key_extra, key_order = jax.random.split(jax.random.fold_in(key, 11))
    extra_draw = jax.random.randint(key_extra, (PARTITIONS, BATCHES, ROWBLOCKS, TILES - 2), 0, 4)
    extra_blocks = jnp.minimum(extra_draw, 1).astype(jnp.int32)
    both_blocks = jnp.broadcast_to(jnp.arange(2, dtype=jnp.int32), (PARTITIONS, BATCHES, ROWBLOCKS, 2))
    blocks_all = jnp.concatenate([both_blocks, extra_blocks], axis=-1)
    priority = jax.random.randint(key_order, (PARTITIONS, BATCHES, ROWBLOCKS, TILES), 0, 1048576) * TILES + jnp.arange(TILES, dtype=jnp.int32)
    shuffle = jnp.argsort(priority, axis=-1)
    return jnp.take_along_axis(blocks_all, shuffle, axis=-1).astype(jnp.int32)


def draw_tile_values(key, part):
    key_mask, key_value = jax.random.split(jax.random.fold_in(key, 23))
    full_shape = (PARTITIONS, BATCHES, ROWBLOCKS, TILES, BLK, BLK)
    kept_mask = jax.random.uniform(key_mask, full_shape) < 0.0625
    values = jax.random.uniform(key_value, full_shape, minval=0.5, maxval=1.5)
    row_scale = 16.0 / (BLK * TILES)
    return jnp.where(kept_mask, values * row_scale, 0.0).astype(jnp.bfloat16)


def set_ends(array, rng, smallest, largest):
    longest = array.shape.index(max(array.shape))
    spots = []
    for shift in (0, 1):
        where = [jax.random.randint(jax.random.fold_in(rng, axis), (), 0, length) for axis, length in enumerate(array.shape)]
        where[longest] = (where[longest] + shift) % array.shape[longest]
        spots.append(tuple(where))
    return array.at[spots[0]].set(smallest).at[spots[1]].set(largest)


def steps_of(own_key, shape, pieces, least, high):
    factor_of, own = 1.0, jax.random.fold_in(own_key, 6)
    for position, shards_of in pieces:
        draws = jnp.exp(jax.random.uniform(jax.random.fold_in(own, position), (shards_of,), jnp.float32, least / len(pieces), high / len(pieces)))
        factor_of = factor_of * jnp.repeat(draws, shape[position] // shards_of).reshape([-1 if axis == position else 1 for axis in range(len(shape))])
    return factor_of


def bell_draw(key, dims, scale, most, shards=(), kind=jnp.bfloat16):
    drawn = scale * jax.random.normal(key, dims, jnp.float32)
    if shards:
        drawn = drawn * steps_of(key, dims, shards, -0.22, 0.18)
    return jnp.clip(drawn, -most, most).astype(kind)


def setup_inputs(seed: int = 0) -> dict:
    streams_of = jax.random.split(jax.random.key(seed), 6)
    return {
        "initial_feat": bell_draw(streams_of[0], (BATCHES, NODES, F), 1.0, 6.0, ((1, 8),)),
        "layer_weight": draw_layer_weight(jax.random.fold_in(streams_of[5], 71), 0),
        "tile_column": draw_tile_column(jax.random.fold_in(streams_of[5], 71), 0),
        "tile_values": draw_tile_values(jax.random.fold_in(streams_of[5], 71), 0),
        "send_rows": set_ends(jax.random.randint(streams_of[4], (PARTITIONS, BATCHES, PARTITIONS, SEND), 0, PART_ROWS), jax.random.fold_in(streams_of[4], 1), 0, PART_ROWS - 1).astype(jnp.int32),
    }


restart = 0.1
strength = 0.5


def boundary_rows(features, picks):
    blocks = features.reshape(PARTITIONS, PART_ROWS, features.shape[-1])
    owners = jnp.arange(PARTITIONS, dtype=jnp.int32)[:, None, None]
    picked = blocks[owners, picks]
    boundary = jnp.transpose(picked, (1, 0, 2, 3)).reshape(PARTITIONS, BLK, features.shape[-1])
    return blocks, boundary


def gcn_layer(features, initial, weight_now, tile_block, tile_weights, picks, layer_num):
    width = features.shape[-1]
    blocks, boundary = boundary_rows(features, picks)
    row_blocks = blocks.reshape(PARTITIONS, ROWBLOCKS, BLK, width)
    own_mask = (tile_block == 0)[..., None, None]
    weights_f = tile_weights.astype(jnp.float32)
    own_weights = jnp.where(own_mask, weights_f, 0.0)
    far_weights = jnp.where(own_mask, 0.0, weights_f)
    own_part = jnp.einsum("drtij,drjf->drif", own_weights, row_blocks.astype(jnp.float32))
    far_part = jnp.einsum("drtij,djf->drif", far_weights, boundary.astype(jnp.float32))
    aggregate = (own_part + far_part).reshape(NODES, width)
    mixed_in = ((1.0 - restart) * aggregate + restart * initial.astype(jnp.float32)).astype(jnp.bfloat16)
    product = jnp.dot(mixed_in, weight_now, preferred_element_type=jnp.float32)
    layer_pos = jnp.float32(layer_num)
    beta_mix = jnp.log(strength / layer_pos + 1.0)
    return jax.nn.relu((1.0 - beta_mix) * mixed_in.astype(jnp.float32) + beta_mix * product).astype(jnp.bfloat16)


def reference(initial_feat, layer_weight, tile_column, tile_values, send_rows):
    per_layer = [[] for layer_num in range(LAYERS)]
    for batch_num in range(BATCHES):
        initial = initial_feat[batch_num]
        features = initial
        for layer_num in range(LAYERS):
            features = gcn_layer(features, initial, layer_weight[layer_num], tile_column[:, batch_num],
                                 tile_values[:, batch_num], send_rows[:, batch_num], layer_num + 1)
            per_layer[layer_num].append(features)
    return jnp.stack([jnp.stack(layer_rows, 0) for layer_rows in per_layer], 0)
```

```python
import functools
import math

import jax
import jax.numpy as jnp
from jax import lax
from jax.experimental import pallas as pl
from jax.experimental.pallas import tpu as pltpu
from jax.sharding import PartitionSpec as P

restart = 0.1
strength = 0.5
VMEM = pl.BlockSpec(memory_space=pltpu.VMEM)
SMEM = pl.BlockSpec(memory_space=pltpu.SMEM)


def params():
    return pltpu.CompilerParams(vmem_limit_bytes=24 * 1024 * 1024)


def pick_matrix(send, rows):
    parts, each = send.shape
    total = parts * each
    line = lax.broadcasted_iota(jnp.int32, (total, parts), 0) // each
    part = lax.broadcasted_iota(jnp.int32, (total, parts), 1)
    spread = jnp.dot(
        (line == part).astype(jnp.float32),
        send.astype(jnp.float32),
        precision=lax.Precision.HIGHEST,
        preferred_element_type=jnp.float32,
    )
    slot = lax.broadcasted_iota(jnp.int32, (total, each), 0) % each
    lane = lax.broadcasted_iota(jnp.int32, (total, each), 1)
    row = jnp.sum(jnp.where(slot == lane, spread, 0.0), axis=1, keepdims=True)
    local = lax.broadcasted_iota(jnp.int32, (total, rows), 1).astype(jnp.float32)
    return (local == row).astype(jnp.bfloat16)


def tile_sums(block_ref, tiles_ref, batch, r):
    own = far = None
    for t in range(tiles_ref.shape[3]):
        tile = tiles_ref[0, batch, r, t].astype(jnp.float32)
        is_own = block_ref[0, batch, r, t] == 0
        own_t = tile * jnp.where(is_own, 1.0, 0.0)
        far_t = tile * jnp.where(is_own, 0.0, 1.0)
        own = own_t if own is None else own + own_t
        far = far_t if far is None else far + far_t
    return jnp.concatenate([own, far], axis=1).astype(jnp.bfloat16)


def first_kernel(group, send_ref, init_ref, pick_ref, out_ref):
    batch = lax.axis_index("section") % group
    pick = pick_matrix(send_ref[0, batch], init_ref.shape[1])
    pick_ref[...] = pick
    out_ref[...] = jnp.dot(
        pick, init_ref[batch], preferred_element_type=jnp.float32
    ).astype(jnp.bfloat16)


def layer_kernel(group, step, from_init, last, *refs):
    block_ref, tiles_ref, init_ref, pick_ref, bound_ref = refs[:5]
    weights = refs[5 : 5 + group]
    rest = refs[5 + group :]
    if from_init:
        current_ref = None
    else:
        current_ref, rest = rest[0], rest[1:]
    if last:
        x_ref, mixed_ref = rest
        out_ref = None
    else:
        x_ref, out_ref, mixed_ref = rest
    section = lax.axis_index("section")
    batch = section % group
    row_blocks, side = tiles_ref.shape[2], tiles_ref.shape[4]
    boundary = bound_ref[...]
    for r in range(row_blocks):
        rows = pl.ds(r * side, side)
        own = init_ref[batch, rows, :] if from_init else current_ref[rows, :]
        both = jnp.concatenate([own, boundary], axis=0)
        aggregate = jnp.dot(
            tile_sums(block_ref, tiles_ref, batch, r), both, preferred_element_type=jnp.float32
        )
        initial = init_ref[batch, rows, :].astype(jnp.float32)
        mixed_ref[rows, :] = ((1.0 - restart) * aggregate + restart * initial).astype(jnp.bfloat16)

    layer = (section // group) * group + step + 1
    beta = jnp.float32(0.0)
    for number in range(step + 1, lax.axis_size("section") + 1, group):
        beta = jnp.where(layer == number, jnp.float32(math.log(strength / number + 1.0)), beta)

    for shift in range(group):

        @pl.when((batch + shift) % group == step)
        def _(weight_ref=weights[shift]):
            mixed = mixed_ref[...]
            product = jnp.dot(mixed, weight_ref[...], preferred_element_type=jnp.float32)
            x = (1.0 - beta) * mixed.astype(jnp.float32) + beta * product
            x_ref[...] = jnp.maximum(x, 0.0).astype(jnp.bfloat16)

    if not last:
        out_ref[...] = jnp.dot(
            pick_ref[...], x_ref[...], preferred_element_type=jnp.float32
        ).astype(jnp.bfloat16)


def on_device(initial_feat, layer_weight, tile_column, tile_values, send_rows):
    section_count = lax.axis_size("section")
    batches, rows, width = initial_feat.shape
    group = batches
    stages = section_count // group
    section = lax.axis_index("section")
    member = section % group
    mine = section // group
    sent = send_rows.shape[2] * send_rows.shape[3]
    bf16 = jnp.bfloat16

    def shifted(x, by):
        pairs = [
            (s, (s // group) * group + (s - by) % group) for s in range(section_count)
        ]
        return lax.ppermute(x, "section", pairs)

    def crossed(x):
        pairs = [(s, s + group) for s in range(section_count - group)]
        return lax.ppermute(x, "section", pairs)

    def exchanged(x):
        return lax.all_to_all(x, "dom", split_axis=0, concat_axis=0, tiled=True)

    own_weight = layer_weight[0]
    weights = [own_weight] + [shifted(own_weight, by) for by in range(1, group)]

    pick, outgoing = pl.pallas_call(
        functools.partial(first_kernel, group),
        out_shape=[
            jax.ShapeDtypeStruct((sent, rows), bf16),
            jax.ShapeDtypeStruct((sent, width), bf16),
        ],
        in_specs=[VMEM, VMEM],
        out_specs=[VMEM, VMEM],
        compiler_params=params(),
        name="first_rows",
    )(send_rows, initial_feat)

    def layer(step, current, boundary, last):
        from_init = current is None
        outs = [jax.ShapeDtypeStruct((rows, width), bf16)]
        if not last:
            outs.append(jax.ShapeDtypeStruct((sent, width), bf16))
        operands = [tile_column, tile_values, initial_feat, pick, boundary] + weights
        if not from_init:
            operands.append(current)
        return pl.pallas_call(
            functools.partial(layer_kernel, group, step, from_init, last),
            out_shape=outs,
            in_specs=[SMEM] + [VMEM] * (len(operands) - 1),
            out_specs=[VMEM] * len(outs),
            scratch_shapes=[pltpu.VMEM((rows, width), bf16)],
            compiler_params=params(),
            name="layer",
        )(*operands)

    boundary = exchanged(outgoing)
    current = None
    kept = None
    for stage in range(stages):
        outs = []
        for step in range(group):
            last = stage == stages - 1 and step == group - 1
            result = layer(step, current, boundary, last)
            current = result[0]
            outs.append(current)
            if last:
                break
            boundary = exchanged(result[1])
        kept = outs if kept is None else [
            jnp.where(mine == stage, new, old) for new, old in zip(outs, kept)
        ]
        if stage < stages - 1:
            current = crossed(current)
            boundary = crossed(boundary)

    stack = jnp.stack(kept)
    pieces = []
    for by in range(group):
        wanted = lax.dynamic_index_in_dim(stack, (member - by) % group, 0, keepdims=False)
        pieces.append(wanted if by == 0 else shifted(wanted, by))
    order = [
        lax.select_n((b - member) % group, *pieces) for b in range(group)
    ]
    return jnp.stack(order)[None]


def solution(mesh):
    in_specs = (
        P(None, "dom", None),
        P("section", None, None),
        P("dom", None, None, None),
        P("dom", None, None, None, None, None),
        P("dom", None, None, None),
    )
    out_specs = P("section", None, "dom", None)
    return jax.shard_map(
        on_device, mesh=mesh, in_specs=in_specs, out_specs=out_specs, check_vma=False
    )
```

```python
import functools
import math

import jax
import jax.numpy as jnp
from jax import lax
from jax.experimental import pallas as pl
from jax.experimental.pallas import tpu as pltpu
from jax.sharding import PartitionSpec as P

restart = 0.1
strength = 0.5
VMEM = pl.BlockSpec(memory_space=pltpu.VMEM)
HBM = pl.BlockSpec(memory_space=pltpu.HBM)
bf16 = jnp.bfloat16
f32 = jnp.float32
MIB = 1024 * 1024


def call(kernel, outs, in_specs, out_specs, scratch=(), aliases=None, cost=None):
    return pl.pallas_call(
        kernel,
        out_shape=[jax.ShapeDtypeStruct(shape, bf16) for shape in outs],
        in_specs=in_specs,
        out_specs=out_specs,
        scratch_shapes=list(scratch),
        input_output_aliases=aliases or {},
        cost_estimate=cost,
        compiler_params=pltpu.CompilerParams(vmem_limit_bytes=16 * MIB),
    )


def pick_matrix(send, rows):
    parts, each = send.shape
    total = parts * each
    line = lax.broadcasted_iota(jnp.int32, (total, parts), 0) // each
    part = lax.broadcasted_iota(jnp.int32, (total, parts), 1)
    spread = jnp.dot(
        (line == part).astype(f32),
        send.astype(f32),
        precision=lax.Precision.HIGHEST,
        preferred_element_type=f32,
    )
    slot = lax.broadcasted_iota(jnp.int32, (total, each), 0) % each
    lane = lax.broadcasted_iota(jnp.int32, (total, each), 1)
    row = jnp.sum(jnp.where(slot == lane, spread, 0.0), axis=1, keepdims=True)
    local = lax.broadcasted_iota(jnp.int32, (total, rows), 1).astype(f32)
    return (local == row).astype(bf16)


def first_kernel(
    group,
    send_hbm,
    block_hbm,
    init_hbm,
    tiles_hbm,
    weight_hbm,
    out_ref,
    pick_ref,
    mix_ref,
    init_ref,
    weight_ref,
    send_ref,
    block_ref,
    tiles_ref,
    sems,
):
    batch = lax.axis_index("section") % group
    copies = [
        pltpu.make_async_copy(source, target, sems.at[i])
        for i, (source, target) in enumerate(
            [
                (send_hbm.at[0, batch], send_ref),
                (init_hbm.at[batch], init_ref),
                (block_hbm.at[0, batch], block_ref),
                (tiles_hbm.at[0, batch], tiles_ref),
            ]
        )
    ]
    count = sems.shape[0] - len(copies)
    part = weight_ref.shape[0] // count
    for i in range(count):
        rows = pl.ds(i * part, part)
        copies.append(
            pltpu.make_async_copy(
                weight_hbm.at[0, rows], weight_ref.at[rows], sems.at[4 + i]
            )
        )
    for copy in copies:
        copy.start()
    copies[0].wait()
    pick = pick_matrix(send_ref[...], init_ref.shape[0])
    pick_ref[...] = pick
    copies[1].wait()
    out_ref[...] = jnp.dot(pick, init_ref[...], preferred_element_type=f32).astype(bf16)
    copies[2].wait()
    copies[3].wait()
    row_blocks, tiles = tiles_ref.shape[:2]
    for r in range(row_blocks):
        own = far = None
        for t in range(tiles):
            tile = tiles_ref[r, t].astype(f32)
            is_own = block_ref[r, t] == 0
            own_t = tile * jnp.where(is_own, 1.0, 0.0)
            far_t = tile * jnp.where(is_own, 0.0, 1.0)
            own = own_t if own is None else own + own_t
            far = far_t if far is None else far + far_t
        mix_ref[r] = jnp.concatenate([own, far], axis=1).astype(bf16)
    for copy in copies[4:]:
        copy.wait()


def layer_kernel(group, stage, step, has_current, has_old, has_x, *refs):
    refs = list(refs)
    mix_ref, init_ref, pick_ref, bound_ref = refs[:4]
    weights = refs[4 : 4 + group]
    refs = refs[4 + group :]
    current_ref = refs.pop(0) if has_current else init_ref
    end = step == group - 1
    earlier = [refs.pop(0) for _ in range(group - 2)] if end else []
    old = [refs.pop(0) for _ in range(group)] if has_old else []
    mixed_ref = refs.pop()
    spare = None if has_x else refs.pop()
    picked = [refs.pop() for _ in range(group)][::-1] if end else []
    if has_x:
        x_ref, out_ref = refs
    else:
        x_ref, out_ref = spare, None

    section = lax.axis_index("section")
    member = section % group
    row_blocks, side = mix_ref.shape[:2]
    boundary = bound_ref[...]
    for r in range(row_blocks):
        rows = pl.ds(r * side, side)
        both = jnp.concatenate([current_ref[rows, :], boundary], axis=0)
        aggregate = jnp.dot(mix_ref[r], both, preferred_element_type=f32)
        initial = init_ref[rows, :].astype(f32)
        mixed_ref[rows, :] = ((1.0 - restart) * aggregate + restart * initial).astype(bf16)

    layer = (section // group) * group + step + 1
    beta = f32(0.0)
    for number in range(step + 1, lax.axis_size("section") + 1, group):
        beta = jnp.where(layer == number, f32(math.log(strength / number + 1.0)), beta)

    for shift in range(group):

        @pl.when((member + shift) % group == step)
        def _(weight_ref=weights[shift]):
            mixed = mixed_ref[...]
            product = jnp.dot(mixed, weight_ref[...], preferred_element_type=f32)
            x = (1.0 - beta) * mixed.astype(f32) + beta * product
            x_ref[...] = jnp.maximum(x, 0.0).astype(bf16)

    if out_ref is not None:
        out_ref[...] = jnp.dot(
            pick_ref[...], x_ref[...], preferred_element_type=f32
        ).astype(bf16)

    if end:
        layers = earlier + ([current_ref] if group > 1 else []) + [x_ref]

        def pick_from(sources):
            for target, source in zip(picked, sources):
                target[...] = source[...]

        for value in range(group):
            here = member == value
            if old:
                here = here & (section // group == stage)

            @pl.when(here)
            def _(value=value):
                pick_from([layers[(value - by) % group] for by in range(group)])

        if old:

            @pl.when(section // group != stage)
            def _():
                pick_from(old)


def write_kernel(group, shifts, *refs):
    pieces = refs[: len(shifts)]
    target, sems = refs[-2:]
    member = lax.axis_index("section") % group
    copies = [
        pltpu.make_async_copy(piece, target.at[0, (member + by) % group], sems.at[i])
        for i, (by, piece) in enumerate(zip(shifts, pieces))
    ]
    for copy in copies:
        copy.start()
    for copy in copies:
        copy.wait()


def on_device(initial_feat, layer_weight, tile_column, tile_values, send_rows):
    section_count = lax.axis_size("section")
    batches, rows, width = initial_feat.shape
    group = batches
    stages = section_count // group
    row_blocks, tiles, side = tile_values.shape[2:5]
    sent = send_rows.shape[2] * send_rows.shape[3]

    def shifted(x, by):
        pairs = [(s, (s // group) * group + (s - by) % group) for s in range(section_count)]
        return lax.ppermute(x, "section", pairs)

    def crossed(x):
        pairs = [(s, s + group) for s in range(section_count - group)]
        return lax.ppermute(x, "section", pairs)

    def exchanged(x):
        return lax.all_to_all(x, "dom", split_axis=0, concat_axis=0, tiled=True)

    def first():
        chunks = 4
        return call(
            functools.partial(first_kernel, group),
            [
                (sent, width),
                (sent, rows),
                (row_blocks, side, 2 * side),
                (rows, width),
                layer_weight.shape[1:],
            ],
            [HBM] * 5,
            [VMEM] * 5,
            [
                pltpu.VMEM(send_rows.shape[2:], jnp.int32),
                pltpu.SMEM((row_blocks, tiles), jnp.int32),
                pltpu.VMEM(tile_values.shape[2:], bf16),
                pltpu.SemaphoreType.DMA((4 + chunks,)),
            ],
        )(
            *[
                pltpu.with_memory_space_constraint(x, pltpu.HBM)
                for x in (send_rows, tile_column, initial_feat, tile_values, layer_weight)
            ]
        )

    def layer(stage, step, shared, boundary, weights, currents, old):
        end = step == group - 1
        has_x = not (end and stage == stages - 1)
        has_current = bool(currents)
        operands = list(shared) + [boundary] + weights
        if has_current:
            operands.append(currents[-1])
        if end:
            operands += currents[-group + 1 : -1]
            operands += old
        outs = [(rows, width), (sent, width)] if has_x else []
        if end:
            outs += [(rows, width)] * group
        scratch = [] if has_x else [pltpu.VMEM((rows, width), bf16)]
        scratch.append(pltpu.VMEM((rows, width), bf16))
        flops = 2 * width * rows * (2 * side + width) + 2 * width * rows * sent
        moved = 2 * width * (width + 3 * rows)
        return call(
            functools.partial(
                layer_kernel, group, stage, step, has_current, end and bool(old), has_x
            ),
            outs,
            [VMEM] * len(operands),
            [VMEM] * len(outs),
            scratch,
            cost=pl.CostEstimate(flops=flops, bytes_accessed=moved, transcendentals=0),
        )(*operands)

    outgoing, pick, mix, init, own_weight = first()
    weights = [own_weight] + [shifted(own_weight, by) for by in range(1, group)]
    boundary = exchanged(outgoing)
    shared = [mix, init, pick]
    current = None
    picked = []
    for stage in range(stages):
        currents = [] if stage == 0 else [current]
        for step in range(group):
            result = layer(stage, step, shared, boundary, weights, currents, picked)
            if step < group - 1:
                currents.append(result[0])
                boundary = exchanged(result[1])
            else:
                picked = result[-group:]
        if stage < stages - 1:
            rows_sent = crossed(result[1])
            current = crossed(result[0])
            boundary = exchanged(rows_sent)

    pieces = [shifted(picked[by], by) for by in range(1, group)]
    shape = (1, batches, rows, width)
    target = call(
        functools.partial(write_kernel, group, [0]),
        [shape],
        [VMEM],
        [HBM],
        [pltpu.SemaphoreType.DMA((1,))],
        cost=pl.CostEstimate(flops=0, bytes_accessed=4 * rows * width, transcendentals=0),
    )(picked[0])[0]
    if group == 1:
        return target
    return call(
        lambda *refs: write_kernel(
            group, range(1, group), *refs[: group - 1], *refs[group:]
        ),
        [shape],
        [VMEM] * (group - 1) + [HBM],
        [HBM],
        [pltpu.SemaphoreType.DMA((group - 1,))],
        aliases={group - 1: 0},
    )(*pieces, target)[0]


def solution(mesh):
    in_specs = (
        P(None, "dom", None),
        P("section", None, None),
        P("dom", None, None, None),
        P("dom", None, None, None, None, None),
        P("dom", None, None, None),
    )
    out_specs = P("section", None, "dom", None)
    return jax.shard_map(
        on_device, mesh=mesh, in_specs=in_specs, out_specs=out_specs, check_vma=False
    )
```

```python
import functools
import math

import jax
import jax.numpy as jnp
import numpy as np
from jax import lax
from jax.experimental import pallas as pl
from jax.experimental.pallas import tpu as pltpu
from jax.sharding import PartitionSpec as P

restart = 0.1
strength = 0.5
VMEM = pl.BlockSpec(memory_space=pltpu.VMEM)
HBM = pl.BlockSpec(memory_space=pltpu.HBM)
bf16 = jnp.bfloat16
f32 = jnp.float32
MIB = 1024 * 1024


def call(kernel, outs, in_specs, out_specs, scratch=(), aliases=None, cost=None):
    return pl.pallas_call(
        kernel,
        out_shape=[jax.ShapeDtypeStruct(shape, bf16) for shape in outs],
        in_specs=in_specs,
        out_specs=out_specs,
        scratch_shapes=list(scratch),
        input_output_aliases=aliases or {},
        cost_estimate=cost,
        compiler_params=pltpu.CompilerParams(vmem_limit_bytes=16 * MIB),
    )


def partner_order(count):
    return [int(i) for i in np.random.RandomState(2756).permutation(count)]


def looked_up(index, table):
    result = jnp.zeros_like(index)
    for i, value in enumerate(table):
        result = jnp.where(index == i, value, result)
    return result


def pick_matrix(send, rows):
    parts, each = send.shape
    total = parts * each
    line = lax.broadcasted_iota(jnp.int32, (total, parts), 0) // each
    line = looked_up(line, partner_order(parts))
    part = lax.broadcasted_iota(jnp.int32, (total, parts), 1)
    spread = jnp.dot(
        (line == part).astype(f32),
        send.astype(f32),
        precision=lax.Precision.HIGHEST,
        preferred_element_type=f32,
    )
    slot = lax.broadcasted_iota(jnp.int32, (total, each), 0) % each
    lane = lax.broadcasted_iota(jnp.int32, (total, each), 1)
    row = jnp.sum(jnp.where(slot == lane, spread, 0.0), axis=1, keepdims=True)
    local = lax.broadcasted_iota(jnp.int32, (total, rows), 1).astype(f32)
    return (local == row).astype(bf16)


def arrival_matrix(parts, each):
    total = parts * each
    here = lax.broadcasted_iota(jnp.int32, (total, total), 1)
    source = looked_up(here // each, partner_order(parts)) * each + here % each
    return (lax.broadcasted_iota(jnp.int32, (total, total), 0) == source).astype(bf16)


def first_kernel(
    group,
    send_hbm,
    block_hbm,
    init_hbm,
    tiles_hbm,
    weight_hbm,
    out_ref,
    pick_ref,
    mix_ref,
    init_ref,
    weight_ref,
    send_ref,
    block_ref,
    tiles_ref,
    sems,
):
    batch = lax.axis_index("section") % group
    copies = [
        pltpu.make_async_copy(source, target, sems.at[i])
        for i, (source, target) in enumerate(
            [
                (send_hbm.at[0, batch], send_ref),
                (init_hbm.at[batch], init_ref),
                (block_hbm.at[0, batch], block_ref),
                (tiles_hbm.at[0, batch], tiles_ref),
            ]
        )
    ]
    count = sems.shape[0] - len(copies)
    part = weight_ref.shape[0] // count
    for i in range(count):
        rows = pl.ds(i * part, part)
        copies.append(
            pltpu.make_async_copy(
                weight_hbm.at[0, rows], weight_ref.at[rows], sems.at[4 + i]
            )
        )
    for copy in copies:
        copy.start()
    copies[0].wait()
    pick = pick_matrix(send_ref[...], init_ref.shape[0])
    pick_ref[...] = pick
    copies[1].wait()
    out_ref[...] = jnp.dot(pick, init_ref[...], preferred_element_type=f32).astype(bf16)
    copies[2].wait()
    copies[3].wait()
    row_blocks, tiles = tiles_ref.shape[:2]
    arrival = arrival_matrix(*send_ref.shape)
    for r in range(row_blocks):
        own = far = None
        for t in range(tiles):
            tile = tiles_ref[r, t].astype(f32)
            is_own = block_ref[r, t] == 0
            own_t = tile * jnp.where(is_own, 1.0, 0.0)
            far_t = tile * jnp.where(is_own, 0.0, 1.0)
            own = own_t if own is None else own + own_t
            far = far_t if far is None else far + far_t
        far = jnp.dot(far.astype(bf16), arrival, preferred_element_type=f32)
        mix_ref[r] = jnp.concatenate([own, far], axis=1).astype(bf16)
    for copy in copies[4:]:
        copy.wait()


def layer_kernel(group, stage, step, has_current, has_old, has_x, *refs):
    refs = list(refs)
    mix_ref, init_ref, pick_ref, bound_ref = refs[:4]
    weights = refs[4 : 4 + group]
    refs = refs[4 + group :]
    current_ref = refs.pop(0) if has_current else init_ref
    end = step == group - 1
    earlier = [refs.pop(0) for _ in range(group - 2)] if end else []
    old = [refs.pop(0) for _ in range(group)] if has_old else []
    mixed_ref = refs.pop()
    spare = None if has_x else refs.pop()
    picked = [refs.pop() for _ in range(group)][::-1] if end else []
    if has_x:
        x_ref, out_ref = refs
    else:
        x_ref, out_ref = spare, None

    section = lax.axis_index("section")
    member = section % group
    row_blocks, side = mix_ref.shape[:2]
    boundary = bound_ref[...]
    for r in range(row_blocks):
        rows = pl.ds(r * side, side)
        both = jnp.concatenate([current_ref[rows, :], boundary], axis=0)
        aggregate = jnp.dot(mix_ref[r], both, preferred_element_type=f32)
        initial = init_ref[rows, :].astype(f32)
        mixed_ref[rows, :] = ((1.0 - restart) * aggregate + restart * initial).astype(bf16)

    layer = (section // group) * group + step + 1
    beta = f32(0.0)
    for number in range(step + 1, lax.axis_size("section") + 1, group):
        beta = jnp.where(layer == number, f32(math.log(strength / number + 1.0)), beta)

    for shift in range(group):

        @pl.when((member + shift) % group == step)
        def _(weight_ref=weights[shift]):
            mixed = mixed_ref[...]
            product = jnp.dot(mixed, weight_ref[...], preferred_element_type=f32)
            x = (1.0 - beta) * mixed.astype(f32) + beta * product
            x_ref[...] = jnp.maximum(x, 0.0).astype(bf16)

    if out_ref is not None:
        out_ref[...] = jnp.dot(
            pick_ref[...], x_ref[...], preferred_element_type=f32
        ).astype(bf16)

    if end:
        layers = earlier + ([current_ref] if group > 1 else []) + [x_ref]

        def pick_from(sources):
            for target, source in zip(picked, sources):
                target[...] = source[...]

        for value in range(group):
            here = member == value
            if old:
                here = here & (section // group == stage)

            @pl.when(here)
            def _(value=value):
                pick_from([layers[(value - by) % group] for by in range(group)])

        if old:

            @pl.when(section // group != stage)
            def _():
                pick_from(old)


def write_kernel(group, shifts, *refs):
    pieces = refs[: len(shifts)]
    target, sems = refs[-2:]
    member = lax.axis_index("section") % group
    copies = [
        pltpu.make_async_copy(piece, target.at[0, (member + by) % group], sems.at[i])
        for i, (by, piece) in enumerate(zip(shifts, pieces))
    ]
    for copy in copies:
        copy.start()
    for copy in copies:
        copy.wait()


def on_device(initial_feat, layer_weight, tile_column, tile_values, send_rows):
    section_count = lax.axis_size("section")
    batches, rows, width = initial_feat.shape
    group = batches
    stages = section_count // group
    row_blocks, tiles, side = tile_values.shape[2:5]
    sent = send_rows.shape[2] * send_rows.shape[3]

    def shifted(x, by):
        pairs = [(s, (s // group) * group + (s - by) % group) for s in range(section_count)]
        return lax.ppermute(x, "section", pairs)

    def crossed(x):
        pairs = [(s, s + group) for s in range(section_count - group)]
        return lax.ppermute(x, "section", pairs)

    parts = lax.axis_size("dom")
    order = partner_order(parts)
    groups = [[s * parts + p for p in order] for s in range(section_count)]

    def exchanged(x):
        return lax.all_to_all(
            x,
            ("section", "dom"),
            split_axis=0,
            concat_axis=0,
            axis_index_groups=groups,
            tiled=True,
        )

    def first():
        chunks = 4
        return call(
            functools.partial(first_kernel, group),
            [
                (sent, width),
                (sent, rows),
                (row_blocks, side, 2 * side),
                (rows, width),
                layer_weight.shape[1:],
            ],
            [HBM] * 5,
            [VMEM] * 5,
            [
                pltpu.VMEM(send_rows.shape[2:], jnp.int32),
                pltpu.SMEM((row_blocks, tiles), jnp.int32),
                pltpu.VMEM(tile_values.shape[2:], bf16),
                pltpu.SemaphoreType.DMA((4 + chunks,)),
            ],
        )(
            *[
                pltpu.with_memory_space_constraint(x, pltpu.HBM)
                for x in (send_rows, tile_column, initial_feat, tile_values, layer_weight)
            ]
        )

    def layer(stage, step, shared, boundary, weights, currents, old):
        end = step == group - 1
        has_x = not (end and stage == stages - 1)
        has_current = bool(currents)
        operands = list(shared) + [boundary] + weights
        if has_current:
            operands.append(currents[-1])
        if end:
            operands += currents[-group + 1 : -1]
            operands += old
        outs = [(rows, width), (sent, width)] if has_x else []
        if end:
            outs += [(rows, width)] * group
        scratch = [] if has_x else [pltpu.VMEM((rows, width), bf16)]
        scratch.append(pltpu.VMEM((rows, width), bf16))
        flops = 2 * width * rows * (2 * side + width) + 2 * width * rows * sent
        moved = 2 * width * (width + 3 * rows)
        return call(
            functools.partial(
                layer_kernel, group, stage, step, has_current, end and bool(old), has_x
            ),
            outs,
            [VMEM] * len(operands),
            [VMEM] * len(outs),
            scratch,
            cost=pl.CostEstimate(flops=flops, bytes_accessed=moved, transcendentals=0),
        )(*operands)

    outgoing, pick, mix, init, own_weight = first()
    weights = [own_weight] + [shifted(own_weight, by) for by in range(1, group)]
    boundary = exchanged(outgoing)
    shared = [mix, init, pick]
    current = None
    picked = []
    for stage in range(stages):
        currents = [] if stage == 0 else [current]
        for step in range(group):
            result = layer(stage, step, shared, boundary, weights, currents, picked)
            if step < group - 1:
                currents.append(result[0])
                boundary = exchanged(result[1])
            else:
                picked = result[-group:]
        if stage < stages - 1:
            rows_sent = crossed(result[1])
            current = crossed(result[0])
            boundary = exchanged(rows_sent)

    pieces = [shifted(picked[by], by) for by in range(1, group)]
    shape = (1, batches, rows, width)
    target = call(
        functools.partial(write_kernel, group, [0]),
        [shape],
        [VMEM],
        [HBM],
        [pltpu.SemaphoreType.DMA((1,))],
        cost=pl.CostEstimate(flops=0, bytes_accessed=4 * rows * width, transcendentals=0),
    )(picked[0])[0]
    if group == 1:
        return target
    return call(
        lambda *refs: write_kernel(
            group, range(1, group), *refs[: group - 1], *refs[group:]
        ),
        [shape],
        [VMEM] * (group - 1) + [HBM],
        [HBM],
        [pltpu.SemaphoreType.DMA((group - 1,))],
        aliases={group - 1: 0},
    )(*pieces, target)[0]


def solution(mesh):
    in_specs = (
        P(None, "dom", None),
        P("section", None, None),
        P("dom", None, None, None),
        P("dom", None, None, None, None, None),
        P("dom", None, None, None),
    )
    out_specs = P("section", None, "dom", None)
    return jax.shard_map(
        on_device, mesh=mesh, in_specs=in_specs, out_specs=out_specs, check_vma=False
    )
```

```python
import functools
import math

import jax
import jax.numpy as jnp
import numpy as np
from jax import lax
from jax.experimental import pallas as pl
from jax.experimental.pallas import tpu as pltpu
from jax.sharding import PartitionSpec as P

restart = 0.1
strength = 0.5
VMEM = pl.BlockSpec(memory_space=pltpu.VMEM)
HBM = pl.BlockSpec(memory_space=pltpu.HBM)
bf16 = jnp.bfloat16
f32 = jnp.float32
MIB = 1024 * 1024


def call(kernel, outs, in_specs, out_specs, scratch=(), aliases=None, cost=None):
    return pl.pallas_call(
        kernel,
        out_shape=[jax.ShapeDtypeStruct(shape, bf16) for shape in outs],
        in_specs=in_specs,
        out_specs=out_specs,
        scratch_shapes=list(scratch),
        input_output_aliases=aliases or {},
        cost_estimate=cost,
        compiler_params=pltpu.CompilerParams(vmem_limit_bytes=16 * MIB),
    )


def partner_order(count):
    return [int(i) for i in np.random.RandomState(2756).permutation(count)]


def looked_up(index, table):
    result = jnp.zeros_like(index)
    for i, value in enumerate(table):
        result = jnp.where(index == i, value, result)
    return result


def pick_matrix(send, rows):
    parts, each = send.shape
    total = parts * each
    line = lax.broadcasted_iota(jnp.int32, (total, parts), 0) // each
    line = looked_up(line, partner_order(parts))
    part = lax.broadcasted_iota(jnp.int32, (total, parts), 1)
    spread = jnp.dot(
        (line == part).astype(f32),
        send.astype(f32),
        precision=lax.Precision.HIGHEST,
        preferred_element_type=f32,
    )
    slot = lax.broadcasted_iota(jnp.int32, (total, each), 0) % each
    lane = lax.broadcasted_iota(jnp.int32, (total, each), 1)
    row = jnp.sum(jnp.where(slot == lane, spread, 0.0), axis=1, keepdims=True)
    local = lax.broadcasted_iota(jnp.int32, (total, rows), 1).astype(f32)
    return (local == row).astype(bf16)


def arrival_matrix(parts, each):
    total = parts * each
    here = lax.broadcasted_iota(jnp.int32, (total, total), 1)
    source = looked_up(here // each, partner_order(parts)) * each + here % each
    return (lax.broadcasted_iota(jnp.int32, (total, total), 0) == source).astype(bf16)


def first_kernel(
    group,
    send_hbm,
    block_hbm,
    init_hbm,
    tiles_hbm,
    out_ref,
    pick_ref,
    mix_ref,
    init_ref,
    send_ref,
    block_ref,
    tiles_ref,
    sems,
):
    batch = lax.axis_index("section") % group
    copies = [
        pltpu.make_async_copy(source, target, sems.at[i])
        for i, (source, target) in enumerate(
            [
                (send_hbm.at[0, batch], send_ref),
                (init_hbm.at[batch], init_ref),
                (block_hbm.at[0, batch], block_ref),
                (tiles_hbm.at[0, batch], tiles_ref),
            ]
        )
    ]
    for copy in copies:
        copy.start()
    copies[0].wait()
    pick = pick_matrix(send_ref[...], init_ref.shape[0])
    pick_ref[...] = pick
    copies[1].wait()
    out_ref[...] = jnp.dot(pick, init_ref[...], preferred_element_type=f32).astype(bf16)
    copies[2].wait()
    copies[3].wait()
    row_blocks, tiles = tiles_ref.shape[:2]
    arrival = arrival_matrix(*send_ref.shape)
    for r in range(row_blocks):
        own = far = None
        for t in range(tiles):
            tile = tiles_ref[r, t].astype(f32)
            is_own = block_ref[r, t] == 0
            own_t = tile * jnp.where(is_own, 1.0, 0.0)
            far_t = tile * jnp.where(is_own, 0.0, 1.0)
            own = own_t if own is None else own + own_t
            far = far_t if far is None else far + far_t
        far = jnp.dot(far.astype(bf16), arrival, preferred_element_type=f32)
        mix_ref[r] = jnp.concatenate([own, far], axis=1).astype(bf16)


def layer_kernel(group, stage, step, has_current, has_old, has_x, *refs):
    refs = list(refs)
    mix_ref, init_ref, pick_ref, bound_ref = refs[:4]
    weights = refs[4 : 4 + group]
    refs = refs[4 + group :]
    current_ref = refs.pop(0) if has_current else init_ref
    end = step == group - 1
    earlier = [refs.pop(0) for _ in range(group - 2)] if end else []
    old = [refs.pop(0) for _ in range(group)] if has_old else []
    mixed_ref = refs.pop()
    spare = None if has_x else refs.pop()
    picked = [refs.pop() for _ in range(group)][::-1] if end else []
    if has_x:
        x_ref, out_ref = refs
    else:
        x_ref, out_ref = spare, None

    section = lax.axis_index("section")
    member = section % group
    row_blocks, side = mix_ref.shape[:2]

    layer = (section // group) * group + step + 1
    beta = f32(0.0)
    for number in range(step + 1, lax.axis_size("section") + 1, group):
        beta = jnp.where(layer == number, f32(math.log(strength / number + 1.0)), beta)

    def body(weight_ref):
        boundary = bound_ref[...]
        for r in range(row_blocks):
            rows = pl.ds(r * side, side)
            both = jnp.concatenate([current_ref[rows, :], boundary], axis=0)
            aggregate = jnp.dot(mix_ref[r], both, preferred_element_type=f32)
            initial = init_ref[rows, :].astype(f32)
            mixed_ref[rows, :] = ((1.0 - restart) * aggregate + restart * initial).astype(bf16)
        mixed = mixed_ref[...]
        product = jnp.dot(mixed, weight_ref[...], preferred_element_type=f32)
        x = (1.0 - beta) * mixed.astype(f32) + beta * product
        x_ref[...] = jnp.maximum(x, 0.0).astype(bf16)
        if out_ref is not None:
            out_ref[...] = jnp.dot(
                pick_ref[...], x_ref[...], preferred_element_type=f32
            ).astype(bf16)

    for shift in range(group):
        pl.when((member + shift) % group == step)(functools.partial(body, weights[shift]))

    if end:
        layers = earlier + ([current_ref] if group > 1 else []) + [x_ref]

        def pick_from(sources):
            for target, source in zip(picked, sources):
                target[...] = source[...]

        for value in range(group):
            here = member == value
            if old:
                here = here & (section // group == stage)

            @pl.when(here)
            def _(value=value):
                pick_from([layers[(value - by) % group] for by in range(group)])

        if old:

            @pl.when(section // group != stage)
            def _():
                pick_from(old)


def write_kernel(group, shifts, *refs):
    pieces = refs[: len(shifts)]
    target, sems = refs[-2:]
    member = lax.axis_index("section") % group
    copies = [
        pltpu.make_async_copy(piece, target.at[0, (member + by) % group], sems.at[i])
        for i, (by, piece) in enumerate(zip(shifts, pieces))
    ]
    for copy in copies:
        copy.start()
    for copy in copies:
        copy.wait()


def on_device(initial_feat, layer_weight, tile_column, tile_values, send_rows):
    section_count = lax.axis_size("section")
    batches, rows, width = initial_feat.shape
    group = batches
    stages = section_count // group
    row_blocks, tiles, side = tile_values.shape[2:5]
    sent = send_rows.shape[2] * send_rows.shape[3]

    def shifted(x, by):
        pairs = [(s, (s // group) * group + (s - by) % group) for s in range(section_count)]
        return lax.ppermute(x, "section", pairs)

    def crossed(x):
        pairs = [(s, s + group) for s in range(section_count - group)]
        return lax.ppermute(x, "section", pairs)

    parts = lax.axis_size("dom")
    order = partner_order(parts)
    groups = [[s * parts + p for p in order] for s in range(section_count)]

    def exchanged(x):
        return lax.all_to_all(
            x,
            ("section", "dom"),
            split_axis=0,
            concat_axis=0,
            axis_index_groups=groups,
            tiled=True,
        )

    def first():
        return call(
            functools.partial(first_kernel, group),
            [
                (sent, width),
                (sent, rows),
                (row_blocks, side, 2 * side),
                (rows, width),
            ],
            [HBM] * 4,
            [VMEM] * 4,
            [
                pltpu.VMEM(send_rows.shape[2:], jnp.int32),
                pltpu.SMEM((row_blocks, tiles), jnp.int32),
                pltpu.VMEM(tile_values.shape[2:], bf16),
                pltpu.SemaphoreType.DMA((4,)),
            ],
        )(
            *[
                pltpu.with_memory_space_constraint(x, pltpu.HBM)
                for x in (send_rows, tile_column, initial_feat, tile_values)
            ]
        )

    def layer(stage, step, shared, boundary, weights, currents, old):
        end = step == group - 1
        has_x = not (end and stage == stages - 1)
        has_current = bool(currents)
        operands = list(shared) + [boundary] + weights
        if has_current:
            operands.append(currents[-1])
        if end:
            operands += currents[-group + 1 : -1]
            operands += old
        outs = [(rows, width), (sent, width)] if has_x else []
        if end:
            outs += [(rows, width)] * group
        scratch = [] if has_x else [pltpu.VMEM((rows, width), bf16)]
        scratch.append(pltpu.VMEM((rows, width), bf16))
        flops = 2 * width * rows * (2 * side + width) + 2 * width * rows * sent
        moved = 2 * width * (width + 3 * rows)
        return call(
            functools.partial(
                layer_kernel, group, stage, step, has_current, end and bool(old), has_x
            ),
            outs,
            [VMEM] * len(operands),
            [VMEM] * len(outs),
            scratch,
            cost=pl.CostEstimate(flops=flops, bytes_accessed=moved, transcendentals=0),
        )(*operands)

    outgoing, pick, mix, init = first()
    weights = [shifted(layer_weight[0], by) for by in range(group)]
    boundary = exchanged(outgoing)
    shared = [mix, init, pick]
    current = None
    picked = []
    for stage in range(stages):
        currents = [] if stage == 0 else [current]
        for step in range(group):
            result = layer(stage, step, shared, boundary, weights, currents, picked)
            if step < group - 1:
                currents.append(result[0])
                boundary = exchanged(result[1])
            else:
                picked = result[-group:]
        if stage < stages - 1:
            rows_sent = crossed(result[1])
            current = crossed(result[0])
            boundary = exchanged(rows_sent)

    pieces = [shifted(picked[by], by) for by in range(1, group)]
    shape = (1, batches, rows, width)
    target = call(
        functools.partial(write_kernel, group, [0]),
        [shape],
        [VMEM],
        [HBM],
        [pltpu.SemaphoreType.DMA((1,))],
        cost=pl.CostEstimate(flops=0, bytes_accessed=4 * rows * width, transcendentals=0),
    )(picked[0])[0]
    if group == 1:
        return target
    return call(
        lambda *refs: write_kernel(
            group, range(1, group), *refs[: group - 1], *refs[group:]
        ),
        [shape],
        [VMEM] * (group - 1) + [HBM],
        [HBM],
        [pltpu.SemaphoreType.DMA((group - 1,))],
        aliases={group - 1: 0},
    )(*pieces, target)[0]


def solution(mesh):
    in_specs = (
        P(None, "dom", None),
        P("section", None, None),
        P("dom", None, None, None),
        P("dom", None, None, None, None, None),
        P("dom", None, None, None),
    )
    out_specs = P("section", None, "dom", None)
    return jax.shard_map(
        on_device, mesh=mesh, in_specs=in_specs, out_specs=out_specs, check_vma=False
    )
```

```python
import functools
import math

import jax
import jax.numpy as jnp
import numpy as np
from jax import lax
from jax.experimental import pallas as pl
from jax.experimental.pallas import tpu as pltpu
from jax.sharding import PartitionSpec as P

restart = 0.1
strength = 0.5
VMEM = pl.BlockSpec(memory_space=pltpu.VMEM)
HBM = pl.BlockSpec(memory_space=pltpu.HBM)
bf16 = jnp.bfloat16
f32 = jnp.float32
MIB = 1024 * 1024


def call(kernel, outs, in_specs, out_specs, scratch=(), aliases=None, cost=None):
    return pl.pallas_call(
        kernel,
        out_shape=[jax.ShapeDtypeStruct(shape, bf16) for shape in outs],
        in_specs=in_specs,
        out_specs=out_specs,
        scratch_shapes=list(scratch),
        input_output_aliases=aliases or {},
        cost_estimate=cost,
        compiler_params=pltpu.CompilerParams(vmem_limit_bytes=16 * MIB),
    )


def partner_order(count):
    return [int(i) for i in np.random.RandomState(2756).permutation(count)]


def looked_up(index, table):
    result = jnp.zeros_like(index)
    for i, value in enumerate(table):
        result = jnp.where(index == i, value, result)
    return result


def pick_matrix(send, rows):
    parts, each = send.shape
    total = parts * each
    line = lax.broadcasted_iota(jnp.int32, (total, parts), 0) // each
    line = looked_up(line, partner_order(parts))
    part = lax.broadcasted_iota(jnp.int32, (total, parts), 1)
    spread = jnp.dot(
        (line == part).astype(f32),
        send.astype(f32),
        precision=lax.Precision.HIGHEST,
        preferred_element_type=f32,
    )
    slot = lax.broadcasted_iota(jnp.int32, (total, each), 0) % each
    lane = lax.broadcasted_iota(jnp.int32, (total, each), 1)
    row = jnp.sum(jnp.where(slot == lane, spread, 0.0), axis=1, keepdims=True)
    local = lax.broadcasted_iota(jnp.int32, (total, rows), 1).astype(f32)
    return (local == row).astype(bf16)


def arrival_matrix(parts, each):
    total = parts * each
    here = lax.broadcasted_iota(jnp.int32, (total, total), 1)
    source = looked_up(here // each, partner_order(parts)) * each + here % each
    return (lax.broadcasted_iota(jnp.int32, (total, total), 0) == source).astype(bf16)


def first_kernel(
    group,
    send_hbm,
    block_hbm,
    init_hbm,
    tiles_hbm,
    weight_hbm,
    out_ref,
    pick_ref,
    mix_ref,
    init_ref,
    weight_ref,
    send_ref,
    block_ref,
    tiles_ref,
    sems,
):
    batch = lax.axis_index("section") % group
    copies = [
        pltpu.make_async_copy(source, target, sems.at[i])
        for i, (source, target) in enumerate(
            [
                (send_hbm.at[0, batch], send_ref),
                (init_hbm.at[batch], init_ref),
                (block_hbm.at[0, batch], block_ref),
                (tiles_hbm.at[0, batch], tiles_ref),
            ]
        )
    ]
    count = sems.shape[0] - len(copies)
    part = weight_ref.shape[0] // count
    for i in range(count):
        rows = pl.ds(i * part, part)
        copies.append(
            pltpu.make_async_copy(
                weight_hbm.at[0, rows], weight_ref.at[rows], sems.at[4 + i]
            )
        )
    for copy in copies:
        copy.start()
    copies[0].wait()
    pick = pick_matrix(send_ref[...], init_ref.shape[0])
    pick_ref[...] = pick
    copies[1].wait()
    out_ref[...] = jnp.dot(pick, init_ref[...], preferred_element_type=f32).astype(bf16)
    copies[2].wait()
    copies[3].wait()
    row_blocks, tiles = tiles_ref.shape[:2]
    arrival = arrival_matrix(*send_ref.shape)
    for r in range(row_blocks):
        own = far = None
        for t in range(tiles):
            tile = tiles_ref[r, t].astype(f32)
            is_own = block_ref[r, t] == 0
            own_t = tile * jnp.where(is_own, 1.0, 0.0)
            far_t = tile * jnp.where(is_own, 0.0, 1.0)
            own = own_t if own is None else own + own_t
            far = far_t if far is None else far + far_t
        far = jnp.dot(far.astype(bf16), arrival, preferred_element_type=f32)
        mix_ref[r] = jnp.concatenate([own, far], axis=1).astype(bf16)
    for copy in copies[4:]:
        copy.wait()


def layer_kernel(group, stage, step, has_current, has_old, has_x, *refs):
    refs = list(refs)
    mix_ref, init_ref, pick_ref, bound_ref = refs[:4]
    weights = refs[4 : 4 + group]
    refs = refs[4 + group :]
    current_ref = refs.pop(0) if has_current else init_ref
    end = step == group - 1
    earlier = [refs.pop(0) for _ in range(group - 2)] if end else []
    old = [refs.pop(0) for _ in range(group)] if has_old else []
    mixed_ref = refs.pop()
    spare = None if has_x else refs.pop()
    picked = [refs.pop() for _ in range(group)][::-1] if end else []
    if has_x:
        x_ref, out_ref = refs
    else:
        x_ref, out_ref = spare, None

    section = lax.axis_index("section")
    member = section % group
    row_blocks, side = mix_ref.shape[:2]

    layer = (section // group) * group + step + 1
    beta = f32(0.0)
    for number in range(step + 1, lax.axis_size("section") + 1, group):
        beta = jnp.where(layer == number, f32(math.log(strength / number + 1.0)), beta)

    def body(weight_ref):
        boundary = bound_ref[...]
        for r in range(row_blocks):
            rows = pl.ds(r * side, side)
            both = jnp.concatenate([current_ref[rows, :], boundary], axis=0)
            aggregate = jnp.dot(mix_ref[r], both, preferred_element_type=f32)
            initial = init_ref[rows, :].astype(f32)
            mixed_ref[rows, :] = ((1.0 - restart) * aggregate + restart * initial).astype(bf16)
        mixed = mixed_ref[...]
        product = jnp.dot(mixed, weight_ref[...], preferred_element_type=f32)
        x = (1.0 - beta) * mixed.astype(f32) + beta * product
        x_ref[...] = jnp.maximum(x, 0.0).astype(bf16)
        if out_ref is not None:
            out_ref[...] = jnp.dot(
                pick_ref[...], x_ref[...], preferred_element_type=f32
            ).astype(bf16)

    active = section // group == stage
    for shift in range(group):
        needed = active & ((member + shift) % group == step)
        pl.when(needed)(functools.partial(body, weights[shift]))

    if end:
        layers = earlier + ([current_ref] if group > 1 else []) + [x_ref]

        def pick_from(sources):
            for target, source in zip(picked, sources):
                target[...] = source[...]

        for value in range(group):
            here = member == value
            if old:
                here = here & (section // group == stage)

            @pl.when(here)
            def _(value=value):
                pick_from([layers[(value - by) % group] for by in range(group)])

        if old:

            @pl.when(section // group != stage)
            def _():
                pick_from(old)


def write_kernel(group, shifts, *refs):
    pieces = refs[: len(shifts)]
    target, sems = refs[-2:]
    member = lax.axis_index("section") % group
    copies = [
        pltpu.make_async_copy(piece, target.at[0, (member + by) % group], sems.at[i])
        for i, (by, piece) in enumerate(zip(shifts, pieces))
    ]
    for copy in copies:
        copy.start()
    for copy in copies:
        copy.wait()


def on_device(initial_feat, layer_weight, tile_column, tile_values, send_rows):
    section_count = lax.axis_size("section")
    batches, rows, width = initial_feat.shape
    group = batches
    stages = section_count // group
    row_blocks, tiles, side = tile_values.shape[2:5]
    sent = send_rows.shape[2] * send_rows.shape[3]

    def shifted(x, by):
        pairs = [(s, (s // group) * group + (s - by) % group) for s in range(section_count)]
        return lax.ppermute(x, "section", pairs)

    def crossed(x):
        pairs = [(s, s + group) for s in range(section_count - group)]
        return lax.ppermute(x, "section", pairs)

    parts = lax.axis_size("dom")
    order = partner_order(parts)
    groups = [[s * parts + p for p in order] for s in range(section_count)]

    def exchanged(x):
        return lax.all_to_all(
            x,
            ("section", "dom"),
            split_axis=0,
            concat_axis=0,
            axis_index_groups=groups,
            tiled=True,
        )

    def first():
        chunks = 4
        return call(
            functools.partial(first_kernel, group),
            [
                (sent, width),
                (sent, rows),
                (row_blocks, side, 2 * side),
                (rows, width),
                layer_weight.shape[1:],
            ],
            [HBM] * 5,
            [VMEM] * 5,
            [
                pltpu.VMEM(send_rows.shape[2:], jnp.int32),
                pltpu.SMEM((row_blocks, tiles), jnp.int32),
                pltpu.VMEM(tile_values.shape[2:], bf16),
                pltpu.SemaphoreType.DMA((4 + chunks,)),
            ],
        )(
            *[
                pltpu.with_memory_space_constraint(x, pltpu.HBM)
                for x in (send_rows, tile_column, initial_feat, tile_values, layer_weight)
            ]
        )

    def layer(stage, step, shared, boundary, weights, currents, old):
        end = step == group - 1
        has_x = not (end and stage == stages - 1)
        has_current = bool(currents)
        operands = list(shared) + [boundary] + weights
        if has_current:
            operands.append(currents[-1])
        if end:
            operands += currents[-group + 1 : -1]
            operands += old
        outs = [(rows, width), (sent, width)] if has_x else []
        if end:
            outs += [(rows, width)] * group
        scratch = [] if has_x else [pltpu.VMEM((rows, width), bf16)]
        scratch.append(pltpu.VMEM((rows, width), bf16))
        flops = 2 * width * rows * (2 * side + width) + 2 * width * rows * sent
        moved = 2 * width * (width + 3 * rows)
        return call(
            functools.partial(
                layer_kernel, group, stage, step, has_current, end and bool(old), has_x
            ),
            outs,
            [VMEM] * len(operands),
            [VMEM] * len(outs),
            scratch,
            cost=pl.CostEstimate(flops=flops, bytes_accessed=moved, transcendentals=0),
        )(*operands)

    outgoing, pick, mix, init, own_weight = first()
    weights = [own_weight] + [shifted(own_weight, by) for by in range(1, group)]
    boundary = exchanged(outgoing)
    shared = [mix, init, pick]
    current = None
    picked = []
    for stage in range(stages):
        currents = [] if stage == 0 else [current]
        for step in range(group):
            result = layer(stage, step, shared, boundary, weights, currents, picked)
            if step < group - 1:
                currents.append(result[0])
                boundary = exchanged(result[1])
            else:
                picked = result[-group:]
        if stage < stages - 1:
            rows_sent = crossed(result[1])
            current = crossed(result[0])
            boundary = exchanged(rows_sent)

    pieces = [shifted(picked[by], by) for by in range(1, group)]
    shape = (1, batches, rows, width)
    target = call(
        functools.partial(write_kernel, group, [0]),
        [shape],
        [VMEM],
        [HBM],
        [pltpu.SemaphoreType.DMA((1,))],
        cost=pl.CostEstimate(flops=0, bytes_accessed=4 * rows * width, transcendentals=0),
    )(picked[0])[0]
    if group == 1:
        return target
    return call(
        lambda *refs: write_kernel(
            group, range(1, group), *refs[: group - 1], *refs[group:]
        ),
        [shape],
        [VMEM] * (group - 1) + [HBM],
        [HBM],
        [pltpu.SemaphoreType.DMA((group - 1,))],
        aliases={group - 1: 0},
    )(*pieces, target)[0]


def solution(mesh):
    in_specs = (
        P(None, "dom", None),
        P("section", None, None),
        P("dom", None, None, None),
        P("dom", None, None, None, None, None),
        P("dom", None, None, None),
    )
    out_specs = P("section", None, "dom", None)
    return jax.shard_map(
        on_device, mesh=mesh, in_specs=in_specs, out_specs=out_specs, check_vma=False
    )
```

```python
import functools
import math

import jax
import jax.numpy as jnp
import numpy as np
from jax import lax
from jax.experimental import pallas as pl
from jax.experimental.pallas import tpu as pltpu
from jax.sharding import PartitionSpec as P

restart = 0.1
strength = 0.5
VMEM = pl.BlockSpec(memory_space=pltpu.VMEM)
HBM = pl.BlockSpec(memory_space=pltpu.HBM)
bf16 = jnp.bfloat16
f32 = jnp.float32
MIB = 1024 * 1024


def call(kernel, outs, in_specs, out_specs, scratch=(), aliases=None, cost=None):
    return pl.pallas_call(
        kernel,
        out_shape=[jax.ShapeDtypeStruct(shape, bf16) for shape in outs],
        in_specs=in_specs,
        out_specs=out_specs,
        scratch_shapes=list(scratch),
        input_output_aliases=aliases or {},
        cost_estimate=cost,
        compiler_params=pltpu.CompilerParams(vmem_limit_bytes=16 * MIB),
    )


def partner_order(count):
    return [int(i) for i in np.random.RandomState(2756).permutation(count)]


def looked_up(index, table):
    result = jnp.zeros_like(index)
    for i, value in enumerate(table):
        result = jnp.where(index == i, value, result)
    return result


def batch_of(section, group):
    return (section % group + section // group) % group


def pick_matrix(send, rows):
    parts, each = send.shape
    total = parts * each
    line = lax.broadcasted_iota(jnp.int32, (total, parts), 0) // each
    line = looked_up(line, partner_order(parts))
    part = lax.broadcasted_iota(jnp.int32, (total, parts), 1)
    spread = jnp.dot(
        (line == part).astype(f32),
        send.astype(f32),
        precision=lax.Precision.HIGHEST,
        preferred_element_type=f32,
    )
    slot = lax.broadcasted_iota(jnp.int32, (total, each), 0) % each
    lane = lax.broadcasted_iota(jnp.int32, (total, each), 1)
    row = jnp.sum(jnp.where(slot == lane, spread, 0.0), axis=1, keepdims=True)
    local = lax.broadcasted_iota(jnp.int32, (total, rows), 1).astype(f32)
    return (local == row).astype(bf16)


def arrival_matrix(parts, each):
    total = parts * each
    here = lax.broadcasted_iota(jnp.int32, (total, total), 1)
    source = looked_up(here // each, partner_order(parts)) * each + here % each
    return (lax.broadcasted_iota(jnp.int32, (total, total), 0) == source).astype(bf16)


def first_kernel(
    group,
    send_hbm,
    block_hbm,
    init_hbm,
    tiles_hbm,
    weight_hbm,
    out_ref,
    pick_ref,
    mix_ref,
    init_ref,
    weight_ref,
    send_ref,
    block_ref,
    tiles_ref,
    sems,
):
    batch = batch_of(lax.axis_index("section"), group)
    copies = [
        pltpu.make_async_copy(source, target, sems.at[i])
        for i, (source, target) in enumerate(
            [
                (send_hbm.at[0, batch], send_ref),
                (init_hbm.at[batch], init_ref),
                (block_hbm.at[0, batch], block_ref),
                (tiles_hbm.at[0, batch], tiles_ref),
            ]
        )
    ]
    count = sems.shape[0] - len(copies)
    part = weight_ref.shape[0] // count
    for i in range(count):
        rows = pl.ds(i * part, part)
        copies.append(
            pltpu.make_async_copy(
                weight_hbm.at[0, rows], weight_ref.at[rows], sems.at[4 + i]
            )
        )
    for copy in copies:
        copy.start()
    copies[0].wait()
    pick = pick_matrix(send_ref[...], init_ref.shape[0])
    pick_ref[...] = pick
    copies[1].wait()
    out_ref[...] = jnp.dot(pick, init_ref[...], preferred_element_type=f32).astype(bf16)
    copies[2].wait()
    copies[3].wait()
    row_blocks, tiles = tiles_ref.shape[:2]
    arrival = arrival_matrix(*send_ref.shape)
    for r in range(row_blocks):
        own = far = None
        for t in range(tiles):
            tile = tiles_ref[r, t].astype(f32)
            is_own = block_ref[r, t] == 0
            own_t = tile * jnp.where(is_own, 1.0, 0.0)
            far_t = tile * jnp.where(is_own, 0.0, 1.0)
            own = own_t if own is None else own + own_t
            far = far_t if far is None else far + far_t
        far = jnp.dot(far.astype(bf16), arrival, preferred_element_type=f32)
        mix_ref[r] = jnp.concatenate([own, far], axis=1).astype(bf16)
    for copy in copies[4:]:
        copy.wait()


def layer_kernel(group, stage, step, has_current, has_old, has_x, *refs):
    refs = list(refs)
    mix_ref, init_ref, pick_ref, bound_ref = refs[:4]
    weights = refs[4 : 4 + group]
    refs = refs[4 + group :]
    current_ref = refs.pop(0) if has_current else init_ref
    end = step == group - 1
    earlier = [refs.pop(0) for _ in range(group - 2)] if end else []
    old = [refs.pop(0) for _ in range(group)] if has_old else []
    mixed_ref = refs.pop()
    spare = None if has_x else refs.pop()
    picked = [refs.pop() for _ in range(group)][::-1] if end else []
    if has_x:
        x_ref, out_ref = refs
    else:
        x_ref, out_ref = spare, None

    section = lax.axis_index("section")
    member = section % group
    row_blocks, side = mix_ref.shape[:2]

    layer = (section // group) * group + step + 1
    beta = f32(0.0)
    for number in range(step + 1, lax.axis_size("section") + 1, group):
        beta = jnp.where(layer == number, f32(math.log(strength / number + 1.0)), beta)

    def body(weight_ref):
        boundary = bound_ref[...]
        for r in range(row_blocks):
            rows = pl.ds(r * side, side)
            both = jnp.concatenate([current_ref[rows, :], boundary], axis=0)
            aggregate = jnp.dot(mix_ref[r], both, preferred_element_type=f32)
            initial = init_ref[rows, :].astype(f32)
            mixed_ref[rows, :] = ((1.0 - restart) * aggregate + restart * initial).astype(bf16)
        mixed = mixed_ref[...]
        product = jnp.dot(mixed, weight_ref[...], preferred_element_type=f32)
        x = (1.0 - beta) * mixed.astype(f32) + beta * product
        x_ref[...] = jnp.maximum(x, 0.0).astype(bf16)
        if out_ref is not None:
            out_ref[...] = jnp.dot(
                pick_ref[...], x_ref[...], preferred_element_type=f32
            ).astype(bf16)

    active = section // group == stage
    for shift in range(group):
        needed = active & ((member + shift) % group == step)
        pl.when(needed)(functools.partial(body, weights[shift]))

    if end:
        layers = earlier + ([current_ref] if group > 1 else []) + [x_ref]

        def pick_from(sources):
            for target, source in zip(picked, sources):
                target[...] = source[...]

        for value in range(group):
            here = member == value
            if old:
                here = here & (section // group == stage)

            @pl.when(here)
            def _(value=value):
                pick_from([layers[(value - by) % group] for by in range(group)])

        if old:

            @pl.when(section // group != stage)
            def _():
                pick_from(old)


def write_kernel(group, shifts, *refs):
    pieces = refs[: len(shifts)]
    target, sems = refs[-2:]
    batch = batch_of(lax.axis_index("section"), group)
    copies = [
        pltpu.make_async_copy(piece, target.at[0, (batch + by) % group], sems.at[i])
        for i, (by, piece) in enumerate(zip(shifts, pieces))
    ]
    for copy in copies:
        copy.start()
    for copy in copies:
        copy.wait()


def on_device(initial_feat, layer_weight, tile_column, tile_values, send_rows):
    section_count = lax.axis_size("section")
    batches, rows, width = initial_feat.shape
    group = batches
    stages = section_count // group
    row_blocks, tiles, side = tile_values.shape[2:5]
    sent = send_rows.shape[2] * send_rows.shape[3]

    def shifted(x, by):
        pairs = [(s, (s // group) * group + (s - by) % group) for s in range(section_count)]
        return lax.ppermute(x, "section", pairs)

    def crossed(x):
        pairs = [
            (s, (s // group + 1) * group + (s - 1) % group) for s in range(section_count - group)
        ]
        return lax.ppermute(x, "section", pairs)

    parts = lax.axis_size("dom")
    order = partner_order(parts)
    groups = [[s * parts + p for p in order] for s in range(section_count)]

    def exchanged(x):
        return lax.all_to_all(
            x,
            ("section", "dom"),
            split_axis=0,
            concat_axis=0,
            axis_index_groups=groups,
            tiled=True,
        )

    def first():
        chunks = 4
        return call(
            functools.partial(first_kernel, group),
            [
                (sent, width),
                (sent, rows),
                (row_blocks, side, 2 * side),
                (rows, width),
                layer_weight.shape[1:],
            ],
            [HBM] * 5,
            [VMEM] * 5,
            [
                pltpu.VMEM(send_rows.shape[2:], jnp.int32),
                pltpu.SMEM((row_blocks, tiles), jnp.int32),
                pltpu.VMEM(tile_values.shape[2:], bf16),
                pltpu.SemaphoreType.DMA((4 + chunks,)),
            ],
        )(
            *[
                pltpu.with_memory_space_constraint(x, pltpu.HBM)
                for x in (send_rows, tile_column, initial_feat, tile_values, layer_weight)
            ]
        )

    def layer(stage, step, shared, boundary, weights, currents, old):
        end = step == group - 1
        has_x = not (end and stage == stages - 1)
        has_current = bool(currents)
        operands = list(shared) + [boundary] + weights
        if has_current:
            operands.append(currents[-1])
        if end:
            operands += currents[-group + 1 : -1]
            operands += old
        outs = [(rows, width), (sent, width)] if has_x else []
        if end:
            outs += [(rows, width)] * group
        scratch = [] if has_x else [pltpu.VMEM((rows, width), bf16)]
        scratch.append(pltpu.VMEM((rows, width), bf16))
        flops = 2 * width * rows * (2 * side + width) + 2 * width * rows * sent
        moved = 2 * width * (width + 3 * rows)
        return call(
            functools.partial(
                layer_kernel, group, stage, step, has_current, end and bool(old), has_x
            ),
            outs,
            [VMEM] * len(operands),
            [VMEM] * len(outs),
            scratch,
            cost=pl.CostEstimate(flops=flops, bytes_accessed=moved, transcendentals=0),
        )(*operands)

    outgoing, pick, mix, init, own_weight = first()
    weights = [own_weight] + [shifted(own_weight, by) for by in range(1, group)]
    boundary = exchanged(outgoing)
    shared = [mix, init, pick]
    current = None
    picked = []
    for stage in range(stages):
        currents = [] if stage == 0 else [current]
        for step in range(group):
            result = layer(stage, step, shared, boundary, weights, currents, picked)
            if step < group - 1:
                currents.append(result[0])
                boundary = exchanged(result[1])
            else:
                picked = result[-group:]
        if stage < stages - 1:
            rows_sent = crossed(result[1])
            current = crossed(result[0])
            boundary = exchanged(rows_sent)

    pieces = [shifted(picked[by], by) for by in range(1, group)]
    shape = (1, batches, rows, width)
    target = call(
        functools.partial(write_kernel, group, [0]),
        [shape],
        [VMEM],
        [HBM],
        [pltpu.SemaphoreType.DMA((1,))],
        cost=pl.CostEstimate(flops=0, bytes_accessed=4 * rows * width, transcendentals=0),
    )(picked[0])[0]
    if group == 1:
        return target
    return call(
        lambda *refs: write_kernel(
            group, range(1, group), *refs[: group - 1], *refs[group:]
        ),
        [shape],
        [VMEM] * (group - 1) + [HBM],
        [HBM],
        [pltpu.SemaphoreType.DMA((group - 1,))],
        aliases={group - 1: 0},
    )(*pieces, target)[0]


def solution(mesh):
    in_specs = (
        P(None, "dom", None),
        P("section", None, None),
        P("dom", None, None, None),
        P("dom", None, None, None, None, None),
        P("dom", None, None, None),
    )
    out_specs = P("section", None, "dom", None)
    return jax.shard_map(
        on_device, mesh=mesh, in_specs=in_specs, out_specs=out_specs, check_vma=False
    )
```

```python
import functools
import math

import jax
import jax.numpy as jnp
import numpy as np
from jax import lax
from jax.experimental import pallas as pl
from jax.experimental.pallas import tpu as pltpu
from jax.sharding import PartitionSpec as P

restart = 0.1
strength = 0.5
VMEM = pl.BlockSpec(memory_space=pltpu.VMEM)
HBM = pl.BlockSpec(memory_space=pltpu.HBM)
bf16 = jnp.bfloat16
f32 = jnp.float32
MIB = 1024 * 1024


def call(kernel, outs, in_specs, out_specs, scratch=(), aliases=None, cost=None):
    return pl.pallas_call(
        kernel,
        out_shape=[jax.ShapeDtypeStruct(shape, bf16) for shape in outs],
        in_specs=in_specs,
        out_specs=out_specs,
        scratch_shapes=list(scratch),
        input_output_aliases=aliases or {},
        cost_estimate=cost,
        compiler_params=pltpu.CompilerParams(vmem_limit_bytes=16 * MIB),
    )


def partner_order(count):
    return [int(i) for i in np.random.RandomState(2756).permutation(count)]


def looked_up(index, table):
    result = jnp.zeros_like(index)
    for i, value in enumerate(table):
        result = jnp.where(index == i, value, result)
    return result


def batch_of(section, group):
    return (section % group + section // group) % group


def pick_matrix(send, rows):
    parts, each = send.shape
    total = parts * each
    line = lax.broadcasted_iota(jnp.int32, (total, parts), 0) // each
    line = looked_up(line, partner_order(parts))
    part = lax.broadcasted_iota(jnp.int32, (total, parts), 1)
    spread = jnp.dot(
        (line == part).astype(f32),
        send.astype(f32),
        precision=lax.Precision.HIGHEST,
        preferred_element_type=f32,
    )
    slot = lax.broadcasted_iota(jnp.int32, (total, each), 0) % each
    lane = lax.broadcasted_iota(jnp.int32, (total, each), 1)
    row = jnp.sum(jnp.where(slot == lane, spread, 0.0), axis=1, keepdims=True)
    local = lax.broadcasted_iota(jnp.int32, (total, rows), 1).astype(f32)
    return (local == row).astype(bf16)


def arrival_matrix(parts, each):
    total = parts * each
    here = lax.broadcasted_iota(jnp.int32, (total, total), 1)
    source = looked_up(here // each, partner_order(parts)) * each + here % each
    return (lax.broadcasted_iota(jnp.int32, (total, total), 0) == source).astype(bf16)


def first_kernel(
    group,
    send_hbm,
    block_hbm,
    init_hbm,
    tiles_hbm,
    weight_hbm,
    out_ref,
    pick_ref,
    mix_ref,
    init_ref,
    weight_ref,
    send_ref,
    block_ref,
    tiles_ref,
    sems,
):
    batch = batch_of(lax.axis_index("section"), group)
    copies = [
        pltpu.make_async_copy(source, target, sems.at[i])
        for i, (source, target) in enumerate(
            [
                (send_hbm.at[0, batch], send_ref),
                (init_hbm.at[batch], init_ref),
                (block_hbm.at[0, batch], block_ref),
                (tiles_hbm.at[0, batch], tiles_ref),
            ]
        )
    ]
    count = sems.shape[0] - len(copies)
    part = weight_ref.shape[0] // count
    for i in range(count):
        rows = pl.ds(i * part, part)
        copies.append(
            pltpu.make_async_copy(
                weight_hbm.at[0, rows], weight_ref.at[rows], sems.at[4 + i]
            )
        )
    for copy in copies:
        copy.start()
    copies[0].wait()
    pick = pick_matrix(send_ref[...], init_ref.shape[0])
    pick_ref[...] = pick
    copies[1].wait()
    out_ref[...] = jnp.dot(pick, init_ref[...], preferred_element_type=f32).astype(bf16)
    copies[2].wait()
    copies[3].wait()
    row_blocks, tiles = tiles_ref.shape[:2]
    arrival = arrival_matrix(*send_ref.shape)
    for r in range(row_blocks):
        own = far = None
        for t in range(tiles):
            tile = tiles_ref[r, t].astype(f32)
            is_own = block_ref[r, t] == 0
            own_t = tile * jnp.where(is_own, 1.0, 0.0)
            far_t = tile * jnp.where(is_own, 0.0, 1.0)
            own = own_t if own is None else own + own_t
            far = far_t if far is None else far + far_t
        far = jnp.dot(far.astype(bf16), arrival, preferred_element_type=f32)
        mix_ref[r] = jnp.concatenate([own, far], axis=1).astype(bf16)
    for copy in copies[4:]:
        copy.wait()


def layer_kernel(group, stage, step, todo, has_current, has_old, *refs):
    refs = list(refs)
    end = step == group - 1
    take = lambda count: [refs.pop(0) for _ in range(count)]
    weights = take(group)
    if todo == "rest":
        (mixed_ref,) = take(1)
        row_blocks = 0
    else:
        mix_ref, init_ref, bound_ref = take(3)
        row_blocks, side = mix_ref.shape[:2]
    pick_ref = take(1)[0] if todo == "rows" or not end else None
    earlier = take(group - 1) if end and todo != "rows" else []
    current_ref = take(1)[0] if has_current and todo != "rest" else None
    old = take(group) if has_old else []
    if todo == "rows":
        mixed_ref, out_ref = take(2)
    else:
        x_ref = take(1)[0]
        out_ref = take(1)[0] if not end else None
        picked = take(group) if end else []
        if todo == "all":
            (mixed_ref,) = take(1)

    section = lax.axis_index("section")
    member = section % group
    layer = (section // group) * group + step + 1
    beta = f32(0.0)
    for number in range(step + 1, lax.axis_size("section") + 1, group):
        beta = jnp.where(layer == number, f32(math.log(strength / number + 1.0)), beta)

    def activated(mixed, weight_ref):
        product = jnp.dot(mixed, weight_ref[...], preferred_element_type=f32)
        x = (1.0 - beta) * mixed.astype(f32) + beta * product
        return jnp.maximum(x, 0.0).astype(bf16)

    def picked_rows(source_ref):
        return jnp.dot(pick_ref[...], source_ref[...], preferred_element_type=f32).astype(bf16)

    def body(weight_ref):
        source_ref = current_ref if has_current else None
        for r in range(row_blocks):
            rows = pl.ds(r * side, side)
            own = init_ref[rows, :] if source_ref is None else source_ref[rows, :]
            both = jnp.concatenate([own, bound_ref[...]], axis=0)
            aggregate = jnp.dot(mix_ref[r], both, preferred_element_type=f32)
            initial = init_ref[rows, :].astype(f32)
            mixed_ref[rows, :] = ((1.0 - restart) * aggregate + restart * initial).astype(bf16)
        if todo == "rows":
            out_ref[...] = activated(picked_rows(mixed_ref), weight_ref)
            return
        x_ref[...] = activated(mixed_ref[...], weight_ref)
        if out_ref is not None:
            out_ref[...] = picked_rows(x_ref)

    active = section // group == stage
    for shift in range(group):
        needed = active & ((member + shift) % group == step)
        pl.when(needed)(functools.partial(body, weights[shift]))

    if end and todo != "rows":
        layers = earlier + [x_ref]

        def pick_from(sources):
            for target, source in zip(picked, sources):
                target[...] = source[...]

        for value in range(group):
            here = active & (member == value) if old else member == value

            @pl.when(here)
            def _(value=value):
                pick_from([layers[(value - by) % group] for by in range(group)])

        if old:

            @pl.when(~active)
            def _():
                pick_from(old)


def write_kernel(group, shifts, *refs):
    pieces = refs[: len(shifts)]
    target, sems = refs[-2:]
    batch = batch_of(lax.axis_index("section"), group)
    copies = [
        pltpu.make_async_copy(piece, target.at[0, (batch + by) % group], sems.at[i])
        for i, (by, piece) in enumerate(zip(shifts, pieces))
    ]
    for copy in copies:
        copy.start()
    for copy in copies:
        copy.wait()


def on_device(initial_feat, layer_weight, tile_column, tile_values, send_rows):
    section_count = lax.axis_size("section")
    batches, rows, width = initial_feat.shape
    group = batches
    stages = section_count // group
    row_blocks, tiles, side = tile_values.shape[2:5]
    sent = send_rows.shape[2] * send_rows.shape[3]

    def shifted(x, by):
        pairs = [(s, (s // group) * group + (s - by) % group) for s in range(section_count)]
        return lax.ppermute(x, "section", pairs)

    def crossed(x):
        pairs = [
            (s, (s // group + 1) * group + (s - 1) % group) for s in range(section_count - group)
        ]
        return lax.ppermute(x, "section", pairs)

    parts = lax.axis_size("dom")
    order = partner_order(parts)
    groups = [[s * parts + p for p in order] for s in range(section_count)]

    def exchanged(x):
        return lax.all_to_all(
            x,
            ("section", "dom"),
            split_axis=0,
            concat_axis=0,
            axis_index_groups=groups,
            tiled=True,
        )

    def first():
        chunks = 4
        return call(
            functools.partial(first_kernel, group),
            [
                (sent, width),
                (sent, rows),
                (row_blocks, side, 2 * side),
                (rows, width),
                layer_weight.shape[1:],
            ],
            [HBM] * 5,
            [VMEM] * 5,
            [
                pltpu.VMEM(send_rows.shape[2:], jnp.int32),
                pltpu.SMEM((row_blocks, tiles), jnp.int32),
                pltpu.VMEM(tile_values.shape[2:], bf16),
                pltpu.SemaphoreType.DMA((4 + chunks,)),
            ],
        )(
            *[
                pltpu.with_memory_space_constraint(x, pltpu.HBM)
                for x in (send_rows, tile_column, initial_feat, tile_values, layer_weight)
            ]
        )

    def layer(stage, step, todo, weights, operands, earlier=(), current=None, old=()):
        end = step == group - 1
        operands = weights + list(operands) + list(earlier)
        if current is not None:
            operands.append(current)
        operands += list(old)
        outs = [(rows, width), (sent, width)]
        scratch = [] if todo == "rest" else [pltpu.VMEM((rows, width), bf16)]
        if todo == "rows":
            scratch = []
        elif end:
            last = stage == stages - 1
            outs = ([] if last else [(rows, width)]) + [(rows, width)] * group
            if last:
                scratch = [pltpu.VMEM((rows, width), bf16)] + scratch
        flops = 2 * width * rows * (2 * side + width) + 2 * width * rows * sent
        moved = 2 * width * (width + 3 * rows)
        kernel = functools.partial(
            layer_kernel, group, stage, step, todo, current is not None, bool(old)
        )

        def reordered(*refs):
            refs = list(refs)
            if end and todo != "rows" and stage == stages - 1:
                place = len(operands)
                x_ref = refs.pop(place + group)
                refs.insert(place, x_ref)
            kernel(*refs)

        return call(
            reordered,
            outs,
            [VMEM] * len(operands),
            [VMEM] * len(outs),
            scratch,
            cost=pl.CostEstimate(flops=flops, bytes_accessed=moved, transcendentals=0),
        )(*operands)

    def opening_exchanged(x):
        x, choice = lax.optimization_barrier((x, opening))
        return lax.cond(
            choice > 0,
            lambda x: exchanged(x),
            jnp.negative,
            x,
        )

    outgoing, pick, mix, init, own_weight = first()
    opening = (lax.axis_index("section") < group).astype(jnp.int32)
    outgoing, opening = lax.optimization_barrier((outgoing, opening))
    weights = [own_weight] + [shifted(own_weight, by) for by in range(1, group)]
    boundary = exchanged(outgoing)
    current = None
    picked = []
    for stage in range(stages):
        earlier = []
        for step in range(group - 1):
            x, outgoing = layer(
                stage, step, "all", weights, [mix, init, boundary, pick], current=current
            )
            earlier.append(x)
            current = x
            if stage == 0:
                boundary = opening_exchanged(outgoing)
            else:
                boundary = exchanged(outgoing)
        step = group - 1
        if stage == stages - 1:
            picked = layer(
                stage, step, "all", weights, [mix, init, boundary], earlier, current, picked
            )
            break
        mixed, outgoing = layer(
            stage, step, "rows", weights, [mix, init, boundary, pick], current=current
        )
        rows_sent = crossed(outgoing)
        x, *picked = layer(
            stage, step, "rest", weights, [mixed], earlier, old=picked
        )
        current = crossed(x)
        boundary = exchanged(rows_sent)

    pieces = [shifted(picked[by], by) for by in range(1, group)]
    shape = (1, batches, rows, width)
    target = call(
        functools.partial(write_kernel, group, [0]),
        [shape],
        [VMEM],
        [HBM],
        [pltpu.SemaphoreType.DMA((1,))],
        cost=pl.CostEstimate(flops=0, bytes_accessed=4 * rows * width, transcendentals=0),
    )(picked[0])[0]
    if group == 1:
        return target
    return call(
        lambda *refs: write_kernel(
            group, range(1, group), *refs[: group - 1], *refs[group:]
        ),
        [shape],
        [VMEM] * (group - 1) + [HBM],
        [HBM],
        [pltpu.SemaphoreType.DMA((group - 1,))],
        aliases={group - 1: 0},
    )(*pieces, target)[0]


def solution(mesh):
    in_specs = (
        P(None, "dom", None),
        P("section", None, None),
        P("dom", None, None, None),
        P("dom", None, None, None, None, None),
        P("dom", None, None, None),
    )
    out_specs = P("section", None, "dom", None)
    return jax.shard_map(
        on_device, mesh=mesh, in_specs=in_specs, out_specs=out_specs, check_vma=False
    )
```

```python
import functools
import math

import jax
import jax.numpy as jnp
import numpy as np
from jax import lax
from jax.experimental import pallas as pl
from jax.experimental.pallas import tpu as pltpu
from jax.sharding import PartitionSpec as P

restart = 0.1
strength = 0.5
VMEM = pl.BlockSpec(memory_space=pltpu.VMEM)
HBM = pl.BlockSpec(memory_space=pltpu.HBM)
bf16 = jnp.bfloat16
f32 = jnp.float32
MIB = 1024 * 1024


def call(kernel, outs, in_specs, out_specs, scratch=(), aliases=None, cost=None):
    return pl.pallas_call(
        kernel,
        out_shape=[jax.ShapeDtypeStruct(shape, bf16) for shape in outs],
        in_specs=in_specs,
        out_specs=out_specs,
        scratch_shapes=list(scratch),
        input_output_aliases=aliases or {},
        cost_estimate=cost,
        compiler_params=pltpu.CompilerParams(vmem_limit_bytes=16 * MIB),
    )


def partner_order(count):
    return [int(i) for i in np.random.RandomState(10814).permutation(count)]


def looked_up(index, table):
    result = jnp.zeros_like(index)
    for i, value in enumerate(table):
        result = jnp.where(index == i, value, result)
    return result


def pick_matrix(send, rows):
    parts, each = send.shape
    total = parts * each
    line = lax.broadcasted_iota(jnp.int32, (total, parts), 0) // each
    line = looked_up(line, partner_order(parts))
    part = lax.broadcasted_iota(jnp.int32, (total, parts), 1)
    spread = jnp.dot(
        (line == part).astype(f32),
        send.astype(f32),
        precision=lax.Precision.HIGHEST,
        preferred_element_type=f32,
    )
    slot = lax.broadcasted_iota(jnp.int32, (total, each), 0) % each
    lane = lax.broadcasted_iota(jnp.int32, (total, each), 1)
    row = jnp.sum(jnp.where(slot == lane, spread, 0.0), axis=1, keepdims=True)
    local = lax.broadcasted_iota(jnp.int32, (total, rows), 1).astype(f32)
    return (local == row).astype(bf16)


def arrival_matrix(parts, each):
    total = parts * each
    here = lax.broadcasted_iota(jnp.int32, (total, total), 1)
    source = looked_up(here // each, partner_order(parts)) * each + here % each
    return (lax.broadcasted_iota(jnp.int32, (total, total), 0) == source).astype(bf16)


def first_kernel(
    group,
    send_hbm,
    block_hbm,
    init_hbm,
    tiles_hbm,
    weight_hbm,
    out_ref,
    pick_ref,
    mix_ref,
    init_ref,
    weight_ref,
    send_ref,
    block_ref,
    tiles_ref,
    sems,
):
    batch = lax.axis_index("section") % group
    copies = [
        pltpu.make_async_copy(source, target, sems.at[i])
        for i, (source, target) in enumerate(
            [
                (send_hbm.at[0, batch], send_ref),
                (init_hbm.at[batch], init_ref),
                (block_hbm.at[0, batch], block_ref),
                (tiles_hbm.at[0, batch], tiles_ref),
            ]
        )
    ]
    count = sems.shape[0] - len(copies)
    part = weight_ref.shape[0] // count
    for i in range(count):
        rows = pl.ds(i * part, part)
        copies.append(
            pltpu.make_async_copy(
                weight_hbm.at[0, rows], weight_ref.at[rows], sems.at[4 + i]
            )
        )
    for copy in copies:
        copy.start()
    copies[0].wait()
    pick = pick_matrix(send_ref[...], init_ref.shape[0])
    pick_ref[...] = pick
    copies[1].wait()
    out_ref[...] = jnp.dot(pick, init_ref[...], preferred_element_type=f32).astype(bf16)
    copies[2].wait()
    copies[3].wait()
    row_blocks, tiles = tiles_ref.shape[:2]
    arrival = arrival_matrix(*send_ref.shape)
    for r in range(row_blocks):
        own = far = None
        for t in range(tiles):
            tile = tiles_ref[r, t].astype(f32)
            is_own = block_ref[r, t] == 0
            own_t = tile * jnp.where(is_own, 1.0, 0.0)
            far_t = tile * jnp.where(is_own, 0.0, 1.0)
            own = own_t if own is None else own + own_t
            far = far_t if far is None else far + far_t
        far = jnp.dot(far.astype(bf16), arrival, preferred_element_type=f32)
        mix_ref[r] = jnp.concatenate([own, far], axis=1).astype(bf16)
    for copy in copies[4:]:
        copy.wait()


def layer_kernel(group, stage, step, todo, has_current, has_old, *refs):
    refs = list(refs)
    end = step == group - 1
    take = lambda count: [refs.pop(0) for _ in range(count)]
    weights = take(group)
    if todo == "rest":
        (mixed_ref,) = take(1)
        row_blocks = 0
    else:
        mix_ref, init_ref, bound_ref = take(3)
        row_blocks, side = mix_ref.shape[:2]
    pick_ref = take(1)[0] if todo == "rows" or not end else None
    earlier = take(group - 1) if end and todo != "rows" else []
    current_ref = take(1)[0] if has_current and todo != "rest" else None
    old = take(group) if has_old else []
    if todo == "rows":
        mixed_ref, out_ref = take(2)
    else:
        x_ref = take(1)[0]
        out_ref = take(1)[0] if not end else None
        picked = take(group) if end else []
        if todo == "all":
            (mixed_ref,) = take(1)

    section = lax.axis_index("section")
    member = section % group
    layer = (section // group) * group + step + 1
    beta = f32(0.0)
    for number in range(step + 1, lax.axis_size("section") + 1, group):
        beta = jnp.where(layer == number, f32(math.log(strength / number + 1.0)), beta)

    def activated(mixed, weight_ref):
        product = jnp.dot(mixed, weight_ref[...], preferred_element_type=f32)
        x = (1.0 - beta) * mixed.astype(f32) + beta * product
        return jnp.maximum(x, 0.0).astype(bf16)

    def picked_rows(source_ref):
        return jnp.dot(pick_ref[...], source_ref[...], preferred_element_type=f32).astype(bf16)

    def body(weight_ref):
        source_ref = current_ref if has_current else None
        for r in range(row_blocks):
            rows = pl.ds(r * side, side)
            own = init_ref[rows, :] if source_ref is None else source_ref[rows, :]
            both = jnp.concatenate([own, bound_ref[...]], axis=0)
            aggregate = jnp.dot(mix_ref[r], both, preferred_element_type=f32)
            initial = init_ref[rows, :].astype(f32)
            mixed_ref[rows, :] = ((1.0 - restart) * aggregate + restart * initial).astype(bf16)
        if todo == "rows":
            out_ref[...] = activated(picked_rows(mixed_ref), weight_ref)
            return
        x_ref[...] = activated(mixed_ref[...], weight_ref)
        if out_ref is not None:
            out_ref[...] = picked_rows(x_ref)

    active = section // group == stage
    for shift in range(group):
        needed = active & ((member + shift) % group == step)
        pl.when(needed)(functools.partial(body, weights[shift]))

    if end and todo != "rows":
        layers = earlier + [x_ref]

        def pick_from(sources):
            for target, source in zip(picked, sources):
                target[...] = source[...]

        for value in range(group):
            here = active & (member == value) if old else member == value

            @pl.when(here)
            def _(value=value):
                pick_from([layers[(value - by) % group] for by in range(group)])

        if old:

            @pl.when(~active)
            def _():
                pick_from(old)


def write_kernel(group, shifts, *refs):
    pieces = refs[: len(shifts)]
    target, sems = refs[-2:]
    member = lax.axis_index("section") % group
    copies = [
        pltpu.make_async_copy(piece, target.at[0, (member + by) % group], sems.at[i])
        for i, (by, piece) in enumerate(zip(shifts, pieces))
    ]
    for copy in copies:
        copy.start()
    for copy in copies:
        copy.wait()


def on_device(initial_feat, layer_weight, tile_column, tile_values, send_rows):
    section_count = lax.axis_size("section")
    batches, rows, width = initial_feat.shape
    group = batches
    stages = section_count // group
    row_blocks, tiles, side = tile_values.shape[2:5]
    sent = send_rows.shape[2] * send_rows.shape[3]

    def shifted(x, by):
        pairs = [(s, (s // group) * group + (s - by) % group) for s in range(section_count)]
        return lax.ppermute(x, "section", pairs)

    def crossed(x):
        pairs = [(s, s + group) for s in range(section_count - group)]
        return lax.ppermute(x, "section", pairs)

    parts = lax.axis_size("dom")
    order = partner_order(parts)
    groups = [[s * parts + p for p in order] for s in range(section_count)]

    def exchanged(x):
        return lax.all_to_all(
            x,
            ("section", "dom"),
            split_axis=0,
            concat_axis=0,
            axis_index_groups=groups,
            tiled=True,
        )

    def first():
        chunks = 8
        return call(
            functools.partial(first_kernel, group),
            [
                (sent, width),
                (sent, rows),
                (row_blocks, side, 2 * side),
                (rows, width),
                layer_weight.shape[1:],
            ],
            [HBM] * 5,
            [VMEM] * 5,
            [
                pltpu.VMEM(send_rows.shape[2:], jnp.int32),
                pltpu.SMEM((row_blocks, tiles), jnp.int32),
                pltpu.VMEM(tile_values.shape[2:], bf16),
                pltpu.SemaphoreType.DMA((4 + chunks,)),
            ],
        )(
            *[
                pltpu.with_memory_space_constraint(x, pltpu.HBM)
                for x in (send_rows, tile_column, initial_feat, tile_values, layer_weight)
            ]
        )

    def layer(stage, step, todo, weights, operands, earlier=(), current=None, old=()):
        end = step == group - 1
        operands = weights + list(operands) + list(earlier)
        if current is not None:
            operands.append(current)
        operands += list(old)
        outs = [(rows, width), (sent, width)]
        scratch = [] if todo == "rest" else [pltpu.VMEM((rows, width), bf16)]
        if todo == "rows":
            scratch = []
        elif end:
            last = stage == stages - 1
            outs = ([] if last else [(rows, width)]) + [(rows, width)] * group
            if last:
                scratch = [pltpu.VMEM((rows, width), bf16)] + scratch
        flops = 2 * width * rows * (2 * side + width) + 2 * width * rows * sent
        moved = 2 * width * (width + 3 * rows)
        kernel = functools.partial(
            layer_kernel, group, stage, step, todo, current is not None, bool(old)
        )

        def reordered(*refs):
            refs = list(refs)
            if end and todo != "rows" and stage == stages - 1:
                place = len(operands)
                x_ref = refs.pop(place + group)
                refs.insert(place, x_ref)
            kernel(*refs)

        return call(
            reordered,
            outs,
            [VMEM] * len(operands),
            [VMEM] * len(outs),
            scratch,
            cost=pl.CostEstimate(flops=flops, bytes_accessed=moved, transcendentals=0),
        )(*operands)

    outgoing, pick, mix, init, own_weight = first()
    weights = [own_weight] + [shifted(own_weight, by) for by in range(1, group)]
    boundary = exchanged(outgoing)
    current = None
    picked = []
    for stage in range(stages):
        earlier = []
        for step in range(group - 1):
            x, outgoing = layer(
                stage, step, "all", weights, [mix, init, boundary, pick], current=current
            )
            earlier.append(x)
            current = x
            boundary = exchanged(outgoing)
        step = group - 1
        if stage == stages - 1:
            picked = layer(
                stage, step, "all", weights, [mix, init, boundary], earlier, current, picked
            )
            break
        mixed, outgoing = layer(
            stage, step, "rows", weights, [mix, init, boundary, pick], current=current
        )
        rows_sent = crossed(outgoing)
        x, *picked = layer(
            stage, step, "rest", weights, [mixed], earlier, old=picked
        )
        current = crossed(x)
        boundary = exchanged(rows_sent)

    pieces = [shifted(picked[by], by) for by in range(1, group)]
    shape = (1, batches, rows, width)
    target = call(
        functools.partial(write_kernel, group, [0]),
        [shape],
        [VMEM],
        [HBM],
        [pltpu.SemaphoreType.DMA((1,))],
        cost=pl.CostEstimate(flops=0, bytes_accessed=4 * rows * width, transcendentals=0),
    )(picked[0])[0]
    if group == 1:
        return target
    return call(
        lambda *refs: write_kernel(
            group, range(1, group), *refs[: group - 1], *refs[group:]
        ),
        [shape],
        [VMEM] * (group - 1) + [HBM],
        [HBM],
        [pltpu.SemaphoreType.DMA((group - 1,))],
        aliases={group - 1: 0},
    )(*pieces, target)[0]


def solution(mesh):
    in_specs = (
        P(None, "dom", None),
        P("section", None, None),
        P("dom", None, None, None),
        P("dom", None, None, None, None, None),
        P("dom", None, None, None),
    )
    out_specs = P("section", None, "dom", None)
    return jax.shard_map(
        on_device, mesh=mesh, in_specs=in_specs, out_specs=out_specs, check_vma=False
    )
```

```python
import functools
import math

import jax
import jax.numpy as jnp
import numpy as np
from jax import lax
from jax.experimental import pallas as pl
from jax.experimental.pallas import tpu as pltpu
from jax.sharding import PartitionSpec as P

restart = 0.1
strength = 0.5
VMEM = pl.BlockSpec(memory_space=pltpu.VMEM)
HBM = pl.BlockSpec(memory_space=pltpu.HBM)
bf16 = jnp.bfloat16
f32 = jnp.float32
MIB = 1024 * 1024
LATE = 5


def call(kernel, outs, in_specs, out_specs, scratch=(), aliases=None, cost=None):
    return pl.pallas_call(
        kernel,
        out_shape=[jax.ShapeDtypeStruct(shape, bf16) for shape in outs],
        in_specs=in_specs,
        out_specs=out_specs,
        scratch_shapes=list(scratch),
        input_output_aliases=aliases or {},
        cost_estimate=cost,
        compiler_params=pltpu.CompilerParams(vmem_limit_bytes=16 * MIB),
    )


def partner_order(count):
    return [int(i) for i in np.random.RandomState(10814).permutation(count)]


def looked_up(index, table):
    result = jnp.zeros_like(index)
    for i, value in enumerate(table):
        result = jnp.where(index == i, value, result)
    return result


def batch_of(section, group):
    return (section % group + section // group) % group


def pick_matrix(send, rows):
    parts, each = send.shape
    total = parts * each
    line = lax.broadcasted_iota(jnp.int32, (total, parts), 0) // each
    line = looked_up(line, partner_order(parts))
    part = lax.broadcasted_iota(jnp.int32, (total, parts), 1)
    spread = jnp.dot(
        (line == part).astype(f32),
        send.astype(f32),
        precision=lax.Precision.HIGHEST,
        preferred_element_type=f32,
    )
    slot = lax.broadcasted_iota(jnp.int32, (total, each), 0) % each
    lane = lax.broadcasted_iota(jnp.int32, (total, each), 1)
    row = jnp.sum(jnp.where(slot == lane, spread, 0.0), axis=1, keepdims=True)
    local = lax.broadcasted_iota(jnp.int32, (total, rows), 1).astype(f32)
    return (local == row).astype(bf16)


def arrival_matrix(parts, each):
    total = parts * each
    here = lax.broadcasted_iota(jnp.int32, (total, total), 1)
    source = looked_up(here // each, partner_order(parts)) * each + here % each
    return (lax.broadcasted_iota(jnp.int32, (total, total), 0) == source).astype(bf16)


def first_kernel(
    group,
    send_hbm,
    block_hbm,
    init_hbm,
    tiles_hbm,
    weight_hbm,
    out_ref,
    pick_ref,
    mix_ref,
    init_ref,
    weight_ref,
    send_ref,
    block_ref,
    tiles_ref,
    sems,
):
    batch = batch_of(lax.axis_index("section"), group)
    copies = [
        pltpu.make_async_copy(source, target, sems.at[i])
        for i, (source, target) in enumerate(
            [
                (send_hbm.at[0, batch], send_ref),
                (init_hbm.at[batch], init_ref),
                (block_hbm.at[0, batch], block_ref),
                (tiles_hbm.at[0, batch], tiles_ref),
            ]
        )
    ]
    count = sems.shape[0] - len(copies)
    part = weight_ref.shape[0] // count
    for i in range(count):
        rows = pl.ds(i * part, part)
        copies.append(
            pltpu.make_async_copy(
                weight_hbm.at[0, rows], weight_ref.at[rows], sems.at[4 + i]
            )
        )
    for copy in copies:
        copy.start()
    copies[0].wait()
    pick = pick_matrix(send_ref[...], init_ref.shape[0])
    pick_ref[...] = pick
    copies[1].wait()
    out_ref[...] = jnp.dot(pick, init_ref[...], preferred_element_type=f32).astype(bf16)
    copies[2].wait()
    copies[3].wait()
    row_blocks, tiles = tiles_ref.shape[:2]
    arrival = arrival_matrix(*send_ref.shape)
    for r in range(row_blocks):
        own = far = None
        for t in range(tiles):
            tile = tiles_ref[r, t].astype(f32)
            is_own = block_ref[r, t] == 0
            own_t = tile * jnp.where(is_own, 1.0, 0.0)
            far_t = tile * jnp.where(is_own, 0.0, 1.0)
            own = own_t if own is None else own + own_t
            far = far_t if far is None else far + far_t
        far = jnp.dot(far.astype(bf16), arrival, preferred_element_type=f32)
        mix_ref[r] = jnp.concatenate([own, far], axis=1).astype(bf16)
    for copy in copies[4:]:
        copy.wait()


def hold_kernel(group, rows_ref, weight_hbm, out_ref, room_ref, sem):
    section = lax.axis_index("section")

    @pl.when((section // group > 0) & (section % group == group - 1))
    def _():
        @pl.loop(0, LATE)
        def _(step):
            copy = pltpu.make_async_copy(weight_hbm.at[0, pl.ds(0, room_ref.shape[0])], room_ref, sem)
            copy.start()
            copy.wait()


def layer_kernel(group, stage, step, todo, has_current, has_old, *refs):
    refs = list(refs)
    end = step == group - 1
    take = lambda count: [refs.pop(0) for _ in range(count)]
    weights = take(group)
    if todo == "rest":
        (mixed_ref,) = take(1)
        row_blocks = 0
    else:
        mix_ref, init_ref, bound_ref = take(3)
        row_blocks, side = mix_ref.shape[:2]
    pick_ref = take(1)[0] if todo == "rows" or not end else None
    earlier = take(group - 1) if end and todo != "rows" else []
    current_ref = take(1)[0] if has_current and todo != "rest" else None
    old = take(group) if has_old else []
    if todo == "rows":
        mixed_ref, out_ref = take(2)
    else:
        x_ref = take(1)[0]
        out_ref = take(1)[0] if not end else None
        picked = take(group) if end else []
        if todo == "all":
            (mixed_ref,) = take(1)

    section = lax.axis_index("section")
    member = section % group
    layer = (section // group) * group + step + 1
    beta = f32(0.0)
    for number in range(step + 1, lax.axis_size("section") + 1, group):
        beta = jnp.where(layer == number, f32(math.log(strength / number + 1.0)), beta)

    def activated(mixed, weight_ref):
        product = jnp.dot(mixed, weight_ref[...], preferred_element_type=f32)
        x = (1.0 - beta) * mixed.astype(f32) + beta * product
        return jnp.maximum(x, 0.0).astype(bf16)

    def picked_rows(source_ref):
        return jnp.dot(pick_ref[...], source_ref[...], preferred_element_type=f32).astype(bf16)

    def body(weight_ref):
        source_ref = current_ref if has_current else None
        for r in range(row_blocks):
            rows = pl.ds(r * side, side)
            own = init_ref[rows, :] if source_ref is None else source_ref[rows, :]
            both = jnp.concatenate([own, bound_ref[...]], axis=0)
            aggregate = jnp.dot(mix_ref[r], both, preferred_element_type=f32)
            initial = init_ref[rows, :].astype(f32)
            mixed_ref[rows, :] = ((1.0 - restart) * aggregate + restart * initial).astype(bf16)
        if todo == "rows":
            out_ref[...] = activated(picked_rows(mixed_ref), weight_ref)
            return
        x_ref[...] = activated(mixed_ref[...], weight_ref)
        if out_ref is not None:
            out_ref[...] = picked_rows(x_ref)

    active = section // group == stage
    for shift in range(group):
        needed = active & ((member + shift) % group == step)
        pl.when(needed)(functools.partial(body, weights[shift]))

    if end and todo != "rows":
        layers = earlier + [x_ref]

        def pick_from(sources):
            for target, source in zip(picked, sources):
                target[...] = source[...]

        for value in range(group):
            here = active & (member == value) if old else member == value

            @pl.when(here)
            def _(value=value):
                pick_from([layers[(value - by) % group] for by in range(group)])

        if old:

            @pl.when(~active)
            def _():
                pick_from(old)


def write_kernel(group, shifts, *refs):
    pieces = refs[: len(shifts)]
    target, sems = refs[-2:]
    batch = batch_of(lax.axis_index("section"), group)
    copies = [
        pltpu.make_async_copy(piece, target.at[0, (batch + by) % group], sems.at[i])
        for i, (by, piece) in enumerate(zip(shifts, pieces))
    ]
    for copy in copies:
        copy.start()
    for copy in copies:
        copy.wait()


def on_device(initial_feat, layer_weight, tile_column, tile_values, send_rows):
    section_count = lax.axis_size("section")
    batches, rows, width = initial_feat.shape
    group = batches
    stages = section_count // group
    row_blocks, tiles, side = tile_values.shape[2:5]
    sent = send_rows.shape[2] * send_rows.shape[3]

    def shifted(x, by):
        pairs = [(s, (s // group) * group + (s - by) % group) for s in range(section_count)]
        return lax.ppermute(x, "section", pairs)

    def crossed(x):
        pairs = [
            (s, (s // group + 1) * group + (s - 1) % group) for s in range(section_count - group)
        ]
        return lax.ppermute(x, "section", pairs)

    parts = lax.axis_size("dom")
    order = partner_order(parts)
    groups = [[s * parts + p for p in order] for s in range(section_count)]

    def exchanged(x):
        return lax.all_to_all(
            x,
            ("section", "dom"),
            split_axis=0,
            concat_axis=0,
            axis_index_groups=groups,
            tiled=True,
        )

    def first():
        chunks = 8
        return call(
            functools.partial(first_kernel, group),
            [
                (sent, width),
                (sent, rows),
                (row_blocks, side, 2 * side),
                (rows, width),
                layer_weight.shape[1:],
            ],
            [HBM] * 5,
            [VMEM] * 5,
            [
                pltpu.VMEM(send_rows.shape[2:], jnp.int32),
                pltpu.SMEM((row_blocks, tiles), jnp.int32),
                pltpu.VMEM(tile_values.shape[2:], bf16),
                pltpu.SemaphoreType.DMA((4 + chunks,)),
            ],
        )(
            *[
                pltpu.with_memory_space_constraint(x, pltpu.HBM)
                for x in (send_rows, tile_column, initial_feat, tile_values, layer_weight)
            ]
        )

    def layer(stage, step, todo, weights, operands, earlier=(), current=None, old=()):
        end = step == group - 1
        operands = weights + list(operands) + list(earlier)
        if current is not None:
            operands.append(current)
        operands += list(old)
        outs = [(rows, width), (sent, width)]
        scratch = [] if todo == "rest" else [pltpu.VMEM((rows, width), bf16)]
        if todo == "rows":
            scratch = []
        elif end:
            last = stage == stages - 1
            outs = ([] if last else [(rows, width)]) + [(rows, width)] * group
            if last:
                scratch = [pltpu.VMEM((rows, width), bf16)] + scratch
        flops = 2 * width * rows * (2 * side + width) + 2 * width * rows * sent
        moved = 2 * width * (width + 3 * rows)
        kernel = functools.partial(
            layer_kernel, group, stage, step, todo, current is not None, bool(old)
        )

        def reordered(*refs):
            refs = list(refs)
            if end and todo != "rows" and stage == stages - 1:
                place = len(operands)
                x_ref = refs.pop(place + group)
                refs.insert(place, x_ref)
            kernel(*refs)

        return call(
            reordered,
            outs,
            [VMEM] * len(operands),
            [VMEM] * len(outs),
            scratch,
            cost=pl.CostEstimate(flops=flops, bytes_accessed=moved, transcendentals=0),
        )(*operands)

    outgoing, pick, mix, init, own_weight = first()
    weights = [own_weight] + [shifted(own_weight, by) for by in range(1, group)]
    outgoing = call(
        functools.partial(hold_kernel, group),
        [(sent, width)],
        [VMEM, HBM],
        [VMEM],
        [pltpu.VMEM((rows, width), bf16), pltpu.SemaphoreType.DMA(())],
        aliases={0: 0},
    )(outgoing, pltpu.with_memory_space_constraint(layer_weight, pltpu.HBM))[0]
    boundary = exchanged(outgoing)
    current = None
    picked = []
    for stage in range(stages):
        earlier = []
        for step in range(group - 1):
            x, outgoing = layer(
                stage, step, "all", weights, [mix, init, boundary, pick], current=current
            )
            earlier.append(x)
            current = x
            boundary = exchanged(outgoing)
        step = group - 1
        if stage == stages - 1:
            picked = layer(
                stage, step, "all", weights, [mix, init, boundary], earlier, current, picked
            )
            break
        mixed, outgoing = layer(
            stage, step, "rows", weights, [mix, init, boundary, pick], current=current
        )
        rows_sent = crossed(outgoing)
        x, *picked = layer(
            stage, step, "rest", weights, [mixed], earlier, old=picked
        )
        current = crossed(x)
        boundary = exchanged(rows_sent)

    pieces = [shifted(picked[by], by) for by in range(1, group)]
    shape = (1, batches, rows, width)
    target = call(
        functools.partial(write_kernel, group, [0]),
        [shape],
        [VMEM],
        [HBM],
        [pltpu.SemaphoreType.DMA((1,))],
        cost=pl.CostEstimate(flops=0, bytes_accessed=4 * rows * width, transcendentals=0),
    )(picked[0])[0]
    if group == 1:
        return target
    return call(
        lambda *refs: write_kernel(
            group, range(1, group), *refs[: group - 1], *refs[group:]
        ),
        [shape],
        [VMEM] * (group - 1) + [HBM],
        [HBM],
        [pltpu.SemaphoreType.DMA((group - 1,))],
        aliases={group - 1: 0},
    )(*pieces, target)[0]


def solution(mesh):
    in_specs = (
        P(None, "dom", None),
        P("section", None, None),
        P("dom", None, None, None),
        P("dom", None, None, None, None, None),
        P("dom", None, None, None),
    )
    out_specs = P("section", None, "dom", None)
    return jax.shard_map(
        on_device, mesh=mesh, in_specs=in_specs, out_specs=out_specs, check_vma=False
    )
```

```python
import functools
import math

import jax
import jax.numpy as jnp
import numpy as np
from jax import lax
from jax.experimental import pallas as pl
from jax.experimental.pallas import tpu as pltpu
from jax.sharding import PartitionSpec as P

restart = 0.1
strength = 0.5
VMEM = pl.BlockSpec(memory_space=pltpu.VMEM)
HBM = pl.BlockSpec(memory_space=pltpu.HBM)
bf16 = jnp.bfloat16
f32 = jnp.float32
MIB = 1024 * 1024
LATE = 5


def call(kernel, outs, in_specs, out_specs, scratch=(), aliases=None, cost=None):
    return pl.pallas_call(
        kernel,
        out_shape=[jax.ShapeDtypeStruct(shape, bf16) for shape in outs],
        in_specs=in_specs,
        out_specs=out_specs,
        scratch_shapes=list(scratch),
        input_output_aliases=aliases or {},
        cost_estimate=cost,
        compiler_params=pltpu.CompilerParams(vmem_limit_bytes=16 * MIB),
    )


def partner_order(count):
    return [int(i) for i in np.random.RandomState(10814).permutation(count)]


def looked_up(index, table):
    result = jnp.zeros_like(index)
    for i, value in enumerate(table):
        result = jnp.where(index == i, value, result)
    return result


def batch_of(section, group):
    return (section % group + section // group) % group


def pick_matrix(send, rows):
    parts, each = send.shape
    total = parts * each
    line = lax.broadcasted_iota(jnp.int32, (total, parts), 0) // each
    line = looked_up(line, partner_order(parts))
    part = lax.broadcasted_iota(jnp.int32, (total, parts), 1)
    spread = jnp.dot(
        (line == part).astype(f32),
        send.astype(f32),
        precision=lax.Precision.HIGHEST,
        preferred_element_type=f32,
    )
    slot = lax.broadcasted_iota(jnp.int32, (total, each), 0) % each
    lane = lax.broadcasted_iota(jnp.int32, (total, each), 1)
    row = jnp.sum(jnp.where(slot == lane, spread, 0.0), axis=1, keepdims=True)
    local = lax.broadcasted_iota(jnp.int32, (total, rows), 1).astype(f32)
    return (local == row).astype(bf16)


def arrival_matrix(parts, each):
    total = parts * each
    here = lax.broadcasted_iota(jnp.int32, (total, total), 1)
    source = looked_up(here // each, partner_order(parts)) * each + here % each
    return (lax.broadcasted_iota(jnp.int32, (total, total), 0) == source).astype(bf16)


def first_kernel(
    group,
    send_hbm,
    block_hbm,
    init_hbm,
    tiles_hbm,
    weight_hbm,
    out_ref,
    pick_ref,
    mix_ref,
    init_ref,
    weight_ref,
    send_ref,
    block_ref,
    tiles_ref,
    sems,
):
    batch = batch_of(lax.axis_index("section"), group)
    copies = [
        pltpu.make_async_copy(source, target, sems.at[i])
        for i, (source, target) in enumerate(
            [
                (send_hbm.at[0, batch], send_ref),
                (init_hbm.at[batch], init_ref),
                (block_hbm.at[0, batch], block_ref),
                (tiles_hbm.at[0, batch], tiles_ref),
            ]
        )
    ]
    count = sems.shape[0] - len(copies)
    part = weight_ref.shape[0] // count
    for i in range(count):
        rows = pl.ds(i * part, part)
        copies.append(
            pltpu.make_async_copy(
                weight_hbm.at[0, rows], weight_ref.at[rows], sems.at[4 + i]
            )
        )
    for copy in copies:
        copy.start()
    copies[0].wait()
    pick = pick_matrix(send_ref[...], init_ref.shape[0])
    pick_ref[...] = pick
    copies[1].wait()
    out_ref[...] = jnp.dot(pick, init_ref[...], preferred_element_type=f32).astype(bf16)
    copies[2].wait()
    copies[3].wait()
    row_blocks, tiles = tiles_ref.shape[:2]
    arrival = arrival_matrix(*send_ref.shape)
    for r in range(row_blocks):
        own = far = None
        for t in range(tiles):
            tile = tiles_ref[r, t].astype(f32)
            is_own = block_ref[r, t] == 0
            own_t = tile * jnp.where(is_own, 1.0, 0.0)
            far_t = tile * jnp.where(is_own, 0.0, 1.0)
            own = own_t if own is None else own + own_t
            far = far_t if far is None else far + far_t
        far = jnp.dot(far.astype(bf16), arrival, preferred_element_type=f32)
        mix_ref[r] = jnp.concatenate([own, far], axis=1).astype(bf16)
    for copy in copies[4:]:
        copy.wait()


def hold_kernel(group, rows_ref, weight_hbm, out_ref, room_ref, sem):
    section = lax.axis_index("section")

    @pl.when((section // group > 0) & (section % group == group - 1))
    def _():
        @pl.loop(0, LATE)
        def _(step):
            copy = pltpu.make_async_copy(weight_hbm.at[0, pl.ds(0, room_ref.shape[0])], room_ref, sem)
            copy.start()
            copy.wait()


def layer_kernel(group, stage, step, todo, has_current, has_old, *refs):
    refs = list(refs)
    end = step == group - 1
    take = lambda count: [refs.pop(0) for _ in range(count)]
    weights = take(group)
    if todo == "rest":
        (mixed_ref,) = take(1)
        row_blocks = 0
    else:
        mix_ref, init_ref, bound_ref = take(3)
        row_blocks, side = mix_ref.shape[:2]
    pick_ref = take(1)[0] if todo == "rows" or not end else None
    earlier = take(group - 1) if end and todo != "rows" else []
    current_ref = take(1)[0] if has_current and todo != "rest" else None
    old = take(group) if has_old else []
    if todo == "rows":
        mixed_ref, out_ref = take(2)
    else:
        x_ref = take(1)[0]
        out_ref = take(1)[0] if not end else None
        shifts = {"send": range(1, group), "keep": [0]}.get(todo, range(group))
        picked = take(len(shifts)) if end else []
        if todo != "rest":
            (mixed_ref,) = take(1)

    section = lax.axis_index("section")
    member = section % group
    layer = (section // group) * group + step + 1
    beta = f32(0.0)
    for number in range(step + 1, lax.axis_size("section") + 1, group):
        beta = jnp.where(layer == number, f32(math.log(strength / number + 1.0)), beta)

    def activated(mixed, weight_ref):
        product = jnp.dot(mixed, weight_ref[...], preferred_element_type=f32)
        x = (1.0 - beta) * mixed.astype(f32) + beta * product
        return jnp.maximum(x, 0.0).astype(bf16)

    def picked_rows(source_ref):
        return jnp.dot(pick_ref[...], source_ref[...], preferred_element_type=f32).astype(bf16)

    def body(weight_ref):
        source_ref = current_ref if has_current else None
        for r in range(row_blocks):
            rows = pl.ds(r * side, side)
            own = init_ref[rows, :] if source_ref is None else source_ref[rows, :]
            both = jnp.concatenate([own, bound_ref[...]], axis=0)
            aggregate = jnp.dot(mix_ref[r], both, preferred_element_type=f32)
            initial = init_ref[rows, :].astype(f32)
            mixed_ref[rows, :] = ((1.0 - restart) * aggregate + restart * initial).astype(bf16)
        if todo == "rows":
            out_ref[...] = activated(picked_rows(mixed_ref), weight_ref)
            return
        x_ref[...] = activated(mixed_ref[...], weight_ref)
        if out_ref is not None:
            out_ref[...] = picked_rows(x_ref)

    active = section // group == stage
    for shift in range(group):
        needed = active & ((member + shift) % group == step)
        if todo == "send":
            needed = needed & (member < group - 1)
        if todo == "keep":
            needed = needed & (member == group - 1)
        pl.when(needed)(functools.partial(body, weights[shift]))

    if end and todo != "rows":
        layers = earlier + [x_ref]

        def pick_from(sources):
            for target, source in zip(picked, sources):
                target[...] = source[...]

        for value in range(group):
            here = active & (member == value) if old else member == value

            @pl.when(here)
            def _(value=value):
                pick_from([layers[(value - by) % group] for by in shifts])

        if old:

            @pl.when(~active)
            def _():
                pick_from([old[by] for by in shifts])


def write_kernel(group, shifts, *refs):
    pieces = refs[: len(shifts)]
    target, sems = refs[-2:]
    batch = batch_of(lax.axis_index("section"), group)
    copies = [
        pltpu.make_async_copy(piece, target.at[0, (batch + by) % group], sems.at[i])
        for i, (by, piece) in enumerate(zip(shifts, pieces))
    ]
    for copy in copies:
        copy.start()
    for copy in copies:
        copy.wait()


def on_device(initial_feat, layer_weight, tile_column, tile_values, send_rows):
    section_count = lax.axis_size("section")
    batches, rows, width = initial_feat.shape
    group = batches
    stages = section_count // group
    row_blocks, tiles, side = tile_values.shape[2:5]
    sent = send_rows.shape[2] * send_rows.shape[3]

    def shifted(x, by):
        pairs = [(s, (s // group) * group + (s - by) % group) for s in range(section_count)]
        return lax.ppermute(x, "section", pairs)

    def crossed(x):
        pairs = [
            (s, (s // group + 1) * group + (s - 1) % group) for s in range(section_count - group)
        ]
        return lax.ppermute(x, "section", pairs)

    parts = lax.axis_size("dom")
    order = partner_order(parts)
    groups = [[s * parts + p for p in order] for s in range(section_count)]

    def exchanged(x):
        return lax.all_to_all(
            x,
            ("section", "dom"),
            split_axis=0,
            concat_axis=0,
            axis_index_groups=groups,
            tiled=True,
        )

    def first():
        chunks = 8
        return call(
            functools.partial(first_kernel, group),
            [
                (sent, width),
                (sent, rows),
                (row_blocks, side, 2 * side),
                (rows, width),
                layer_weight.shape[1:],
            ],
            [HBM] * 5,
            [VMEM] * 5,
            [
                pltpu.VMEM(send_rows.shape[2:], jnp.int32),
                pltpu.SMEM((row_blocks, tiles), jnp.int32),
                pltpu.VMEM(tile_values.shape[2:], bf16),
                pltpu.SemaphoreType.DMA((4 + chunks,)),
            ],
        )(
            *[
                pltpu.with_memory_space_constraint(x, pltpu.HBM)
                for x in (send_rows, tile_column, initial_feat, tile_values, layer_weight)
            ]
        )

    def layer(stage, step, todo, weights, operands, earlier=(), current=None, old=()):
        end = step == group - 1
        operands = weights + list(operands) + list(earlier)
        if current is not None:
            operands.append(current)
        operands += list(old)
        outs = [(rows, width), (sent, width)]
        scratch = [] if todo == "rest" else [pltpu.VMEM((rows, width), bf16)]
        if todo == "rows":
            scratch = []
        elif end:
            last = stage == stages - 1
            count = {"send": group - 1, "keep": 1}.get(todo, group)
            outs = ([] if last else [(rows, width)]) + [(rows, width)] * count
            if last:
                scratch = [pltpu.VMEM((rows, width), bf16)] + scratch
        flops = 2 * width * rows * (2 * side + width) + 2 * width * rows * sent
        moved = 2 * width * (width + 3 * rows)
        kernel = functools.partial(
            layer_kernel, group, stage, step, todo, current is not None, bool(old)
        )

        def reordered(*refs):
            refs = list(refs)
            if end and todo != "rows" and stage == stages - 1:
                place = len(operands)
                x_ref = refs.pop(place + count)
                refs.insert(place, x_ref)
            kernel(*refs)

        return call(
            reordered,
            outs,
            [VMEM] * len(operands),
            [VMEM] * len(outs),
            scratch,
            cost=pl.CostEstimate(flops=flops, bytes_accessed=moved, transcendentals=0),
        )(*operands)

    outgoing, pick, mix, init, own_weight = first()
    weights = [own_weight] + [shifted(own_weight, by) for by in range(1, group)]
    outgoing = call(
        functools.partial(hold_kernel, group),
        [(sent, width)],
        [VMEM, HBM],
        [VMEM],
        [pltpu.VMEM((rows, width), bf16), pltpu.SemaphoreType.DMA(())],
        aliases={0: 0},
    )(outgoing, pltpu.with_memory_space_constraint(layer_weight, pltpu.HBM))[0]
    boundary = exchanged(outgoing)
    current = None
    picked = []
    for stage in range(stages):
        earlier = []
        for step in range(group - 1):
            x, outgoing = layer(
                stage, step, "all", weights, [mix, init, boundary, pick], current=current
            )
            earlier.append(x)
            current = x
            boundary = exchanged(outgoing)
        step = group - 1
        if stage == stages - 1:
            sending, keeping = [
                functools.partial(
                    layer, stage, step, todo, weights, [mix, init, boundary], earlier, current
                )
                for todo in ("send", "keep")
            ]
            to_send = sending(picked)
            break
        mixed, outgoing = layer(
            stage, step, "rows", weights, [mix, init, boundary, pick], current=current
        )
        rows_sent = crossed(outgoing)
        x, *picked = layer(
            stage, step, "rest", weights, [mixed], earlier, old=picked
        )
        current = crossed(x)
        boundary = exchanged(rows_sent)

    pieces = [shifted(piece, by) for by, piece in enumerate(to_send, 1)]
    kept = keeping(picked)
    return call(
        functools.partial(write_kernel, group, range(group)),
        [(1, batches, rows, width)],
        [VMEM] * group,
        [HBM],
        [pltpu.SemaphoreType.DMA((group,))],
    )(*kept, *pieces)[0]


def solution(mesh):
    in_specs = (
        P(None, "dom", None),
        P("section", None, None),
        P("dom", None, None, None),
        P("dom", None, None, None, None, None),
        P("dom", None, None, None),
    )
    out_specs = P("section", None, "dom", None)
    return jax.shard_map(
        on_device, mesh=mesh, in_specs=in_specs, out_specs=out_specs, check_vma=False
    )
```

```python
import functools
import math

import jax
import jax.numpy as jnp
import numpy as np
from jax import lax
from jax.experimental import pallas as pl
from jax.experimental.pallas import tpu as pltpu
from jax.sharding import PartitionSpec as P

restart = 0.1
strength = 0.5
VMEM = pl.BlockSpec(memory_space=pltpu.VMEM)
HBM = pl.BlockSpec(memory_space=pltpu.HBM)
bf16 = jnp.bfloat16
f32 = jnp.float32
MIB = 1024 * 1024
LATE = 5


def call(kernel, outs, in_specs, out_specs, scratch=(), aliases=None, cost=None):
    return pl.pallas_call(
        kernel,
        out_shape=[jax.ShapeDtypeStruct(shape, bf16) for shape in outs],
        in_specs=in_specs,
        out_specs=out_specs,
        scratch_shapes=list(scratch),
        input_output_aliases=aliases or {},
        cost_estimate=cost,
        compiler_params=pltpu.CompilerParams(vmem_limit_bytes=16 * MIB),
    )


def partner_order(count):
    return [int(i) for i in np.random.RandomState(10814).permutation(count)]


def looked_up(index, table):
    result = jnp.zeros_like(index)
    for i, value in enumerate(table):
        result = jnp.where(index == i, value, result)
    return result


def batch_of(section, group):
    return (section % group + section // group) % group


def pick_matrix(send, rows):
    parts, each = send.shape
    total = parts * each
    line = lax.broadcasted_iota(jnp.int32, (total, parts), 0) // each
    line = looked_up(line, partner_order(parts))
    part = lax.broadcasted_iota(jnp.int32, (total, parts), 1)
    spread = jnp.dot(
        (line == part).astype(f32),
        send.astype(f32),
        precision=lax.Precision.HIGHEST,
        preferred_element_type=f32,
    )
    slot = lax.broadcasted_iota(jnp.int32, (total, each), 0) % each
    lane = lax.broadcasted_iota(jnp.int32, (total, each), 1)
    row = jnp.sum(jnp.where(slot == lane, spread, 0.0), axis=1, keepdims=True)
    local = lax.broadcasted_iota(jnp.int32, (total, rows), 1).astype(f32)
    return (local == row).astype(bf16)


def arrival_matrix(parts, each):
    total = parts * each
    here = lax.broadcasted_iota(jnp.int32, (total, total), 1)
    source = looked_up(here // each, partner_order(parts)) * each + here % each
    return (lax.broadcasted_iota(jnp.int32, (total, total), 0) == source).astype(bf16)


def first_kernel(
    group,
    send_hbm,
    block_hbm,
    init_hbm,
    tiles_hbm,
    weight_hbm,
    out_ref,
    pick_ref,
    mix_ref,
    init_ref,
    weight_ref,
    send_ref,
    block_ref,
    tiles_ref,
    sems,
):
    batch = batch_of(lax.axis_index("section"), group)
    copies = [
        pltpu.make_async_copy(source, target, sems.at[i])
        for i, (source, target) in enumerate(
            [
                (send_hbm.at[0, batch], send_ref),
                (init_hbm.at[batch], init_ref),
                (block_hbm.at[0, batch], block_ref),
                (tiles_hbm.at[0, batch], tiles_ref),
            ]
        )
    ]
    count = sems.shape[0] - len(copies)
    part = weight_ref.shape[0] // count
    for i in range(count):
        rows = pl.ds(i * part, part)
        copies.append(
            pltpu.make_async_copy(
                weight_hbm.at[0, rows], weight_ref.at[rows], sems.at[4 + i]
            )
        )
    for copy in copies:
        copy.start()
    copies[0].wait()
    pick = pick_matrix(send_ref[...], init_ref.shape[0])
    pick_ref[...] = pick
    copies[1].wait()
    out_ref[...] = jnp.dot(pick, init_ref[...], preferred_element_type=f32).astype(bf16)
    copies[2].wait()
    copies[3].wait()
    row_blocks, tiles = tiles_ref.shape[:2]
    arrival = arrival_matrix(*send_ref.shape)
    for r in range(row_blocks):
        own = far = None
        for t in range(tiles):
            tile = tiles_ref[r, t].astype(f32)
            is_own = block_ref[r, t] == 0
            own_t = tile * jnp.where(is_own, 1.0, 0.0)
            far_t = tile * jnp.where(is_own, 0.0, 1.0)
            own = own_t if own is None else own + own_t
            far = far_t if far is None else far + far_t
        far = jnp.dot(far.astype(bf16), arrival, preferred_element_type=f32)
        mix_ref[r] = jnp.concatenate([own, far], axis=1).astype(bf16)
    for copy in copies[4:]:
        copy.wait()


def hold_kernel(group, rows_ref, weight_hbm, out_ref, room_ref, sem):
    section = lax.axis_index("section")

    @pl.when((section // group > 0) & (section % group == group - 1))
    def _():
        @pl.loop(0, LATE)
        def _(step):
            copy = pltpu.make_async_copy(weight_hbm.at[0, pl.ds(0, room_ref.shape[0])], room_ref, sem)
            copy.start()
            copy.wait()


def layer_kernel(group, stage, step, todo, has_current, has_old, *refs):
    refs = list(refs)
    end = step == group - 1
    take = lambda count: [refs.pop(0) for _ in range(count)]
    weights = take(group)
    if todo == "rest":
        (mixed_ref,) = take(1)
        row_blocks = 0
    else:
        mix_ref, init_ref, bound_ref = take(3)
        row_blocks, side = mix_ref.shape[:2]
    pick_ref = take(1)[0] if todo == "rows" or not end else None
    earlier = take(group - 1) if end and todo != "rows" else []
    current_ref = take(1)[0] if has_current and todo != "rest" else None
    old = take(group) if has_old else []
    if todo == "rows":
        mixed_ref, out_ref = take(2)
    else:
        x_ref = take(1)[0]
        out_ref = take(1)[0] if not end else None
        shifts = {"send": range(1, group), "keep": [0]}.get(todo, range(group))
        picked = take(len(shifts)) if end else []
        if todo != "rest":
            (mixed_ref,) = take(1)

    section = lax.axis_index("section")
    member = section % group
    layer = (section // group) * group + step + 1
    beta = f32(0.0)
    for number in range(step + 1, lax.axis_size("section") + 1, group):
        beta = jnp.where(layer == number, f32(math.log(strength / number + 1.0)), beta)

    def activated(mixed, weight_ref):
        product = jnp.dot(mixed, weight_ref[...], preferred_element_type=f32)
        x = (1.0 - beta) * mixed.astype(f32) + beta * product
        return jnp.maximum(x, 0.0).astype(bf16)

    def picked_rows(source_ref):
        return jnp.dot(pick_ref[...], source_ref[...], preferred_element_type=f32).astype(bf16)

    def body(weight_ref):
        source_ref = current_ref if has_current else None
        for r in range(row_blocks):
            rows = pl.ds(r * side, side)
            own = init_ref[rows, :] if source_ref is None else source_ref[rows, :]
            both = jnp.concatenate([own, bound_ref[...]], axis=0)
            aggregate = jnp.dot(mix_ref[r], both, preferred_element_type=f32)
            initial = init_ref[rows, :].astype(f32)
            mixed_ref[rows, :] = ((1.0 - restart) * aggregate + restart * initial).astype(bf16)
        if todo == "rows":
            out_ref[...] = activated(picked_rows(mixed_ref), weight_ref)
            return
        x_ref[...] = activated(mixed_ref[...], weight_ref)
        if out_ref is not None:
            out_ref[...] = picked_rows(x_ref)

    active = section // group == stage
    for shift in range(group):
        needed = active & ((member + shift) % group == step)
        if todo == "send":
            needed = needed & (member < group - 1)
        if todo == "keep":
            needed = needed & (member == group - 1)
        pl.when(needed)(functools.partial(body, weights[shift]))

    if end and todo != "rows":
        layers = earlier + [x_ref]

        def pick_from(sources):
            for target, source in zip(picked, sources):
                target[...] = source[...]

        for value in range(group):
            here = active & (member == value) if old else member == value

            @pl.when(here)
            def _(value=value):
                pick_from([layers[(value - by) % group] for by in shifts])

        if old:

            @pl.when(~active)
            def _():
                pick_from([old[by] for by in shifts])


def write_kernel(group, shifts, *refs):
    pieces = refs[: len(shifts)]
    target, sems = refs[-2:]
    batch = batch_of(lax.axis_index("section"), group)
    copies = [
        pltpu.make_async_copy(piece, target.at[0, (batch + by) % group], sems.at[i])
        for i, (by, piece) in enumerate(zip(shifts, pieces))
    ]
    for copy in copies:
        copy.start()
    for copy in copies:
        copy.wait()


def on_device(initial_feat, layer_weight, tile_column, tile_values, send_rows):
    section_count = lax.axis_size("section")
    batches, rows, width = initial_feat.shape
    group = batches
    stages = section_count // group
    row_blocks, tiles, side = tile_values.shape[2:5]
    sent = send_rows.shape[2] * send_rows.shape[3]

    def shifted(x, by):
        pairs = [(s, (s // group) * group + (s - by) % group) for s in range(section_count)]
        return lax.ppermute(x, "section", pairs)

    def crossed(x):
        pairs = [
            (s, (s // group + 1) * group + (s - 1) % group) for s in range(section_count - group)
        ]
        return lax.ppermute(x, "section", pairs)

    parts = lax.axis_size("dom")
    order = partner_order(parts)
    groups = [[s * parts + p for p in order] for s in range(section_count)]

    def exchanged(x):
        return lax.all_to_all(
            x,
            ("section", "dom"),
            split_axis=0,
            concat_axis=0,
            axis_index_groups=groups,
            tiled=True,
        )

    def first():
        chunks = 8
        return call(
            functools.partial(first_kernel, group),
            [
                (sent, width),
                (sent, rows),
                (row_blocks, side, 2 * side),
                (rows, width),
                layer_weight.shape[1:],
            ],
            [HBM] * 5,
            [VMEM] * 5,
            [
                pltpu.VMEM(send_rows.shape[2:], jnp.int32),
                pltpu.SMEM((row_blocks, tiles), jnp.int32),
                pltpu.VMEM(tile_values.shape[2:], bf16),
                pltpu.SemaphoreType.DMA((4 + chunks,)),
            ],
        )(
            *[
                pltpu.with_memory_space_constraint(x, pltpu.HBM)
                for x in (send_rows, tile_column, initial_feat, tile_values, layer_weight)
            ]
        )

    def layer(stage, step, todo, weights, operands, earlier=(), current=None, old=()):
        end = step == group - 1
        operands = weights + list(operands) + list(earlier)
        if current is not None:
            operands.append(current)
        operands += list(old)
        outs = [(rows, width), (sent, width)]
        scratch = [] if todo == "rest" else [pltpu.VMEM((rows, width), bf16)]
        if todo == "rows":
            scratch = []
        elif end:
            last = stage == stages - 1
            count = {"send": group - 1, "keep": 1}.get(todo, group)
            outs = ([] if last else [(rows, width)]) + [(rows, width)] * count
            if last:
                scratch = [pltpu.VMEM((rows, width), bf16)] + scratch
        flops = 2 * width * rows * (2 * side + width) + 2 * width * rows * sent
        moved = 2 * width * (width + 3 * rows)
        kernel = functools.partial(
            layer_kernel, group, stage, step, todo, current is not None, bool(old)
        )

        def reordered(*refs):
            refs = list(refs)
            if end and todo != "rows" and stage == stages - 1:
                place = len(operands)
                x_ref = refs.pop(place + count)
                refs.insert(place, x_ref)
            kernel(*refs)

        return call(
            reordered,
            outs,
            [VMEM] * len(operands),
            [VMEM] * len(outs),
            scratch,
            cost=pl.CostEstimate(flops=flops, bytes_accessed=moved, transcendentals=0),
        )(*operands)

    outgoing, pick, mix, init, own_weight = first()
    weights = [own_weight] + [shifted(own_weight, by) for by in range(1, group)]
    outgoing = call(
        functools.partial(hold_kernel, group),
        [(sent, width)],
        [VMEM, HBM],
        [VMEM],
        [pltpu.VMEM((rows, width), bf16), pltpu.SemaphoreType.DMA(())],
        aliases={0: 0},
    )(outgoing, pltpu.with_memory_space_constraint(layer_weight, pltpu.HBM))[0]
    boundary = exchanged(outgoing)
    current = None
    picked = []
    for stage in range(stages):
        earlier = []
        for step in range(group - 1):
            x, outgoing = layer(
                stage, step, "all", weights, [mix, init, boundary, pick], current=current
            )
            earlier.append(x)
            current = x
            boundary = exchanged(outgoing)
        step = group - 1
        if stage == stages - 1:
            sending, keeping = [
                functools.partial(
                    layer, stage, step, todo, weights, [mix, init, boundary], earlier, current
                )
                for todo in ("send", "keep")
            ]
            to_send = sending(picked)
            break
        mixed, outgoing = layer(
            stage, step, "rows", weights, [mix, init, boundary, pick], current=current
        )
        rows_sent = crossed(outgoing)
        x, *picked = layer(
            stage, step, "rest", weights, [mixed], earlier, old=picked
        )
        current = crossed(x)
        boundary = exchanged(rows_sent)

    pieces = [shifted(piece, by) for by, piece in enumerate(to_send, 1)]
    kept = keeping(picked)
    shape = (1, batches, rows, width)
    target = call(
        functools.partial(write_kernel, group, [0]),
        [shape],
        [VMEM],
        [HBM],
        [pltpu.SemaphoreType.DMA((1,))],
    )(*kept)[0]
    return call(
        lambda *refs: write_kernel(
            group, range(1, group), *refs[: group - 1], *refs[group:]
        ),
        [shape],
        [VMEM] * (group - 1) + [HBM],
        [HBM],
        [pltpu.SemaphoreType.DMA((group - 1,))],
        aliases={group - 1: 0},
    )(*pieces, target)[0]


def solution(mesh):
    in_specs = (
        P(None, "dom", None),
        P("section", None, None),
        P("dom", None, None, None),
        P("dom", None, None, None, None, None),
        P("dom", None, None, None),
    )
    out_specs = P("section", None, "dom", None)
    return jax.shard_map(
        on_device, mesh=mesh, in_specs=in_specs, out_specs=out_specs, check_vma=False
    )
```
